32 devices in a mesh: site: 8 (over z, x), task: 4 (over y, core).
Axes of the slice: x: 2, y: 2, z: 4, core: 2. Of those that a mesh axis runs over, the one named last changes fastest.
Arguments:
- values: bfloat16 [1024, 65536], P('task', 'site'), may hold values from -6 to 6
- factors: bfloat16 [1024, 128], P('task'), may hold values from -0.1875 to 0.1875
- jitter: bfloat16 [2, 65536], P(None, 'site'), may hold values from 0 to 1
- length_scales: float32 [4], replicated, may hold values from 1.1 to 2.5
- nugget: float32 [1024], P('task'), may hold values from 0.1 to 1
- neighbours: int32 [256, 3], P('site'), may hold values from -1 to 255, as said below
Outputs:
- product: float32 [1024, 65536], P('task', 'site')
The draws below stay inside these ranges and needn't reach their ends.
Inputs may be any that keep to these rules, and one draw needn't show every extreme that they name: `neighbours`: row a is (a, (a - 1) mod 256, (a + 1) mod 256), where an entry is -1 if a barrier separates the two tiles; a barrier between tiles a and (a + 1) mod 256 removes each from the other's row.
All inputs are finite; a program needn't handle non-finite values.
Results may differ from the reference program's by a relative error of at most 0.0034.
Values may be sent and summed in bfloat16 or wider, within the bound.
No kernel may reach another device: no remote copies, remote signals or barrier semaphores. Data moves between devices by JAX's collectives and lax.ppermute only.
A program may use at most 64 MiB of HBM per device.

```python
import math
import jax
import jax.numpy as jnp
from jax import lax

TASKS = 1024
Q = 4
R = 32
SIDE = 16
TILE = 256
TILES = 256
SITES = 65536
RANKS = 128


def draw_neighbours(key, part):
    key_bits, key_spot = jax.random.split(key)
    boundary = jnp.arange(TILES, dtype=jnp.int32)
    random_walls = jax.random.randint(key_bits, (TILES,), 0, 4) == 0
    forced_spot = jax.random.randint(key_spot, (), 0, TILES - 2)
    closed = (random_walls | (boundary == forced_spot)) & (boundary != TILES - 2)
    left_tile = (boundary - 1) % TILES
    right_tile = (boundary + 1) % TILES
    left_column = jnp.where(closed[left_tile], -1, left_tile)
    right_column = jnp.where(closed[boundary], -1, right_tile)
    return jnp.stack([boundary, left_column, right_column], axis=1).astype(jnp.int32)


def level_of(key, shape, shards, low, high):
    factor_of = 1.0
    for axis_at, parts in shards:
        steps = jax.random.uniform(jax.random.fold_in(jax.random.fold_in(key, 6), axis_at), (parts,), jnp.float32, low / len(shards), high / len(shards))
        factor_of = factor_of * jnp.repeat(jnp.exp(steps), shape[axis_at] // parts).reshape((-1,) + (1,) * (len(shape) - 1 - axis_at))
    return factor_of


def normal_values(stream_key, dims, width, most, cuts=(), kind=jnp.bfloat16):
    drawn = jax.random.normal(stream_key, dims, jnp.float32) * width
    if len(cuts) > 0:
        drawn = level_of(stream_key, dims, cuts, -0.22, 0.18) * drawn
    return jnp.clip(drawn, min=-most, max=most).astype(kind)


def setup_inputs(seed: int = 0) -> dict:
    keys = jax.random.split(jax.random.key(seed), 7)
    return {
        "values": normal_values(keys[0], (TASKS, SITES), 1.0, 6.0, ((0, 4), (1, 8))),
        "factors": normal_values(keys[1], (TASKS, RANKS), TASKS ** -0.5, 0.1875, ((0, 4),)),
        "jitter": jnp.clip(1.0 * jax.random.uniform(keys[2], (2, SITES), jnp.float32) ** level_of(keys[2], (2, SITES), ((1, 8),), -0.2, 0.2), 0.0, 1.0).astype(jnp.bfloat16),
        "length_scales": jnp.clip(jnp.exp(jax.random.uniform(keys[3], (Q,), jnp.float32, math.log(1.1), math.log(2.5))), 1.1, 2.5),
        "nugget": jnp.clip(jnp.exp(math.log(1.0) - 2.3025851 * jax.random.uniform(keys[4], (TASKS,), jnp.float32) ** level_of(keys[4], (TASKS,), ((0, 4),), -0.2, 0.2)), 0.1, 1.0),
        "neighbours": draw_neighbours(jax.random.fold_in(keys[6], 71), 0),
    }


def make_kernel(tile_shift, present, own_jitter, far_jitter, scales):
    positions = jnp.arange(TILE, dtype=jnp.int32)
    grid_rows = (positions // SIDE).astype(jnp.float32)
    grid_cols = (positions % SIDE).astype(jnp.float32)
    far_across = far_jitter[0].astype(jnp.float32) + grid_rows
    far_side = far_jitter[1].astype(jnp.float32) + grid_cols
    own_across = own_jitter[0].astype(jnp.float32) + grid_rows
    own_side = own_jitter[1].astype(jnp.float32) + grid_cols
    across = (tile_shift * SIDE).astype(jnp.float32)[:, :, None, None] + far_across[:, :, None, :] - own_across[:, None, :, None]
    sideways = far_side[:, :, None, :] - own_side[:, None, :, None]
    distance = across * across + sideways * sideways
    scaled = distance[None] / (scales * scales)[:, None, None, None, None]
    inside = jnp.maximum(1.0 - scaled, 0.0)
    weight = inside * inside * inside * (1.0 + 3.0 * scaled) * present[None, :, :, None, None]
    return weight.astype(jnp.bfloat16)


def reference(values, factors, jitter, length_scales, nugget, neighbours):
    projected = lax.dot_general(factors, values, (((0,), (0,)), ((), ())), preferred_element_type=jnp.float32).astype(jnp.bfloat16)
    proj_tiles = projected.reshape(Q, R, TILES, TILE)
    jitter_tiles = jitter.reshape(2, TILES, TILE)

    def one_tile(tile_id):
        listed = neighbours[tile_id][None, :].astype(jnp.int32)
        valid = listed >= 0
        safe_ids = jnp.where(valid, listed, tile_id).astype(jnp.int32)
        shifts = ((safe_ids - tile_id + TILES // 2) % TILES) - TILES // 2
        own_jitter = jitter_tiles[:, tile_id][:, None, :]
        far_jitter = jitter_tiles[:, safe_ids]
        kernel = make_kernel(shifts, valid.astype(jnp.float32), own_jitter, far_jitter, length_scales)
        pieces = proj_tiles[:, :, safe_ids]
        smoothed_tile = jnp.einsum("gbkij,grbkj->grbi", kernel.astype(jnp.float32), pieces.astype(jnp.float32))
        return smoothed_tile[:, :, 0, :]

    blocks = lax.map(one_tile, jnp.arange(TILES, dtype=jnp.int32))
    smoothed = blocks.transpose(1, 2, 0, 3).reshape(Q * R, TILES * TILE).astype(jnp.bfloat16)
    mixed = jnp.dot(factors, smoothed, preferred_element_type=jnp.float32)
    return mixed + nugget[:, None] * values.astype(jnp.float32)
```

```python
import jax
import jax.numpy as jnp
from jax import lax
from jax.experimental import pallas as pl
from jax.experimental.pallas import tpu as pltpu
from jax.sharding import PartitionSpec as P

SIDE = 16
TILE = 256
GROUP = 128
HALF = GROUP // 2
REACH = 3 * SIDE
KAPPA = 3.0**-0.25
FAR_AWAY = 1024.0
STEP = 512
EDGE_ROWS = 16
MIB = 1 << 20

VM = pl.BlockSpec(memory_space=pltpu.VMEM)
SM = pl.BlockSpec(memory_space=pltpu.SMEM)
ANY = pl.BlockSpec(memory_space=pl.ANY)


def shape(dims, kind):
    return jax.ShapeDtypeStruct(dims, kind)


def grant(mib):
    return pltpu.CompilerParams(vmem_limit_bytes=mib * MIB)


def cost(flops, size):
    return pl.CostEstimate(flops=flops, bytes_accessed=size, transcendentals=0)


def project(values, factors, core):
    tasks, ranks = factors.shape
    half, width = ranks // 2, values.shape[1]
    steps = width // STEP

    def body(core_ref, f_ref, v_hbm, own_ref, send_ref, v_buf, p_buf, sems):
        spans = [pl.ds(i * STEP, STEP) for i in range(steps)]
        copies = [pltpu.make_async_copy(v_hbm.at[:, s], v_buf.at[:, s], sems.at[i]) for i, s in enumerate(spans)]
        for copy in copies:
            copy.start()
        mine = pl.multiple_of(core_ref[0] * half, half)
        other = pl.multiple_of((1 - core_ref[0]) * half, half)
        turned = f_ref[...].astype(jnp.float32).T.astype(jnp.bfloat16)
        for copy, s in zip(copies, spans):
            copy.wait()
            p_buf[:, s] = jnp.dot(turned, v_buf[:, s], preferred_element_type=jnp.float32)
            own_ref[:, s] = p_buf[pl.ds(mine, half), s]
            send_ref[:, s] = p_buf[pl.ds(other, half), s].astype(jnp.bfloat16)

    return pl.pallas_call(
        body,
        out_shape=(shape((half, width), jnp.float32), shape((half, width), jnp.bfloat16)),
        in_specs=[SM, VM, ANY],
        out_specs=(VM, VM),
        scratch_shapes=[
            pltpu.VMEM((tasks, width), values.dtype),
            pltpu.VMEM((ranks, width), jnp.float32),
            pltpu.SemaphoreType.DMA((steps,)),
        ],
        compiler_params=grant(14),
        cost_estimate=cost(2 * tasks * ranks * width, tasks * width * 2),
        name="project",
    )(core, factors, values)


def add_cores(own, received, jitter, chunks):
    half, width = own.shape
    edge = half + EDGE_ROWS

    def body(own_ref, got_ref, j_ref, *outs):
        for (begin, end), out in zip(chunks, outs):
            s = slice(begin * GROUP, end * GROUP)
            out[...] = (own_ref[:, s] + got_ref[:, s].astype(jnp.float32)).astype(jnp.bfloat16)
        for out, source, s in (
            (outs[-2], outs[0], slice(0, GROUP)),
            (outs[-1], outs[len(chunks) - 1], slice(-GROUP, None)),
        ):
            out[:half, :] = source[:, s]
            out[half:, :] = jnp.zeros((EDGE_ROWS, GROUP), jnp.bfloat16)
            out[half : half + 2, :] = j_ref[:, s]

    return pl.pallas_call(
        body,
        out_shape=[shape((half, (e - b) * GROUP), jnp.bfloat16) for b, e in chunks] + [shape((edge, GROUP), jnp.bfloat16)] * 2,
        in_specs=[VM, VM, VM],
        out_specs=[VM] * (len(chunks) + 2),
        compiler_params=grant(6),
        cost_estimate=cost(half * width, half * width * 8),
        name="add_cores",
    )(own, received, jitter)


def kernel_blocks(jitter, edges, neighbours, scales, core, region, groups, lat):
    begin, end = region
    near = GROUP + REACH
    far = 2 * GROUP - REACH
    half_rows = edges.shape[0] - EDGE_ROWS if edges is not None else 0

    def body(core_ref, near_ref, scale_ref, j_ref, *rest):
        k_ref = rest[-1]
        lane = lax.broadcasted_iota(jnp.int32, (8, 2 * GROUP), 1)
        sub = lax.broadcasted_iota(jnp.int32, (8, 2 * GROUP), 0)
        position = jnp.where(lane < GROUP + HALF, lane, lane - 2 * GROUP)
        row = (position >> 4).astype(jnp.float32)
        col = (position & (SIDE - 1)).astype(jnp.float32)
        mixed_lane = lax.broadcasted_iota(jnp.int32, (2, GROUP), 1)
        own_lane = lax.broadcasted_iota(jnp.int32, (8, GROUP), 1)
        own_sub = lax.broadcasted_iota(jnp.int32, (8, GROUP), 0)
        own_row = (own_lane >> 4).astype(jnp.float32)
        own_col = (own_lane & (SIDE - 1)).astype(jnp.float32)
        betas = []
        for q in range(lat):
            scale = jnp.full((8, GROUP), scale_ref[core_ref[0] * lat + q], jnp.float32)
            betas.append((1.0 / (KAPPA * scale * scale))[:1])

        def offsets(b):
            return j_ref[:, pl.ds(pl.multiple_of(b * GROUP, GROUP), GROUP)].astype(jnp.float32)

        def block(b, first=False, last=False):
            outside = rest[0][half_rows : half_rows + 2, :].astype(jnp.float32) if first or last else None
            here = offsets(b)
            before = outside if first else offsets(b - 1)
            after = outside if last else offsets(b + 1)
            there = jnp.concatenate([here, jnp.where(mixed_lane < HALF, after, before)], axis=1)
            tile, odd = b // 2, lax.rem(b, 2)
            left_gap = jnp.where((odd == 0) & (near_ref[tile, 1] < 0), FAR_AWAY, 0.0)
            right_gap = jnp.where((odd == 1) & (near_ref[tile, 2] < 0), FAR_AWAY, 0.0)
            gap = jnp.where(lane < GROUP, 0.0, jnp.where(lane < GROUP + HALF, right_gap, left_gap))
            pairs = []
            for axis, base, own_base in ((0, row, own_row), (1, col, own_col)):
                there_8 = jnp.broadcast_to(there[axis : axis + 1], (8, 2 * GROUP))
                here_8 = jnp.broadcast_to(here[axis : axis + 1], (8, GROUP))
                extra = gap if axis == 0 else jnp.zeros_like(gap)
                ones = jnp.where(sub < 5, 1.0, 0.0)
                left = jnp.where(sub == 0, there_8, jnp.where(sub == 1, base, jnp.where(sub == 2, extra, ones)))
                right = jnp.where(own_sub < 3, 1.0, jnp.where(own_sub == 3, -here_8, jnp.where(own_sub == 4, -own_base, 0.0)))
                pairs.append((left.T.astype(jnp.bfloat16), right.astype(jnp.bfloat16)))
            slot = b - begin
            for low, high in ((0, near), (far, 2 * GROUP)):
                across, sideways = (jnp.dot(l[low:high], r, preferred_element_type=jnp.float32) for l, r in pairs)
                distance = across * across + sideways * sideways
                for q in range(lat):
                    u = jnp.maximum(1.0 / KAPPA - betas[q] * distance, 0.0)
                    weight = u * u * u * (4.0 * KAPPA**3 - u)
                    k_ref[slot, low:high, q * GROUP : (q + 1) * GROUP] = weight.astype(jnp.bfloat16)
            k_ref[slot, near:far, :] = jnp.zeros((far - near, lat * GROUP), jnp.bfloat16)

        low, high = begin, end
        if begin == 0:
            block(0, first=True)
            low = 1
        if end == groups:
            block(groups - 1, last=True)
            high = groups - 1
        count = 4
        whole = (high - low) // count

        def several(i, carry):
            for m in range(count):
                block(low + i * count + m)
            return carry

        lax.fori_loop(0, whole, several, 0)
        for b in range(low + whole * count, high):
            block(b)

    size = (end - begin) * 2 * GROUP * lat * GROUP
    args = [core, neighbours, scales, jitter] + ([edges] if edges is not None else [])
    return pl.pallas_call(
        body,
        out_shape=shape((end - begin, 2 * GROUP, lat * GROUP), jnp.bfloat16),
        in_specs=[SM, SM, SM] + [VM] * (len(args) - 3),
        out_specs=VM,
        compiler_params=grant(6),
        cost_estimate=cost(30 * size, 2 * size),
        name="kernel_blocks",
    )(*args)


def smooth(blocks, region, pieces, lat, rank):
    begin, end = region
    half = lat * rank

    def body(k_ref, *refs):
        out = refs[-1]
        first_half = lax.broadcasted_iota(jnp.int32, (1, GROUP), 1) < HALF

        def part(group, which, rows):
            for n, (low, high, _) in enumerate(pieces):
                if low <= group < high:
                    return refs[2 * n + which][rows, (group - low) * GROUP : (group - low + 1) * GROUP]

        for b in range(begin, end):
            for q in range(lat):
                rows = slice(q * rank, (q + 1) * rank)
                sides = [
                    jnp.concatenate(
                        [part(b, w, rows), jnp.where(first_half, part(b + 1, w, rows), part(b - 1, w, rows))], axis=1
                    )
                    for w in range(2)
                ]
                total = jnp.dot(
                    jnp.concatenate(sides, axis=0),
                    k_ref[b - begin, :, q * GROUP : (q + 1) * GROUP],
                    preferred_element_type=jnp.float32,
                )
                out[rows, (b - begin) * GROUP : (b - begin + 1) * GROUP] = (total[:rank] + total[rank:]).astype(jnp.bfloat16)

    arrays = [a for _, _, pair in pieces for a in pair]
    count = (end - begin) * GROUP
    return pl.pallas_call(
        body,
        out_shape=shape((half, count), jnp.bfloat16),
        in_specs=[VM] * (1 + len(arrays)),
        out_specs=VM,
        compiler_params=grant(8),
        cost_estimate=cost(8 * half * GROUP * count, 4 * GROUP * lat * count),
        name="smooth",
    )(blocks, *arrays)


def mix(own, received, factors, nugget, values, product, core, region):
    tasks, ranks = factors.shape
    half = ranks // 2
    first, width = region[0] * GROUP, (region[1] - region[0]) * GROUP
    steps = width // STEP

    def body(core_ref, own_ref, got_ref, f_ref, g_ref, v_hbm, *rest):
        o_hbm, v_buf, o_buf, s_buf, in_sems, out_sems = rest[-6:]
        spans = [pl.ds(i * STEP, STEP) for i in range(steps)]
        places = [pl.ds(first + i * STEP, STEP) for i in range(steps)]
        reads = [pltpu.make_async_copy(v_hbm.at[:, p], v_buf.at[:, s], in_sems.at[i]) for i, (s, p) in enumerate(zip(spans, places))]
        writes = [pltpu.make_async_copy(o_buf.at[:, s], o_hbm.at[:, p], out_sems.at[i]) for i, (s, p) in enumerate(zip(spans, places))]
        for copy in reads:
            copy.start()
        s_buf[pl.ds(pl.multiple_of(core_ref[0] * half, half), half), :] = own_ref[...]
        s_buf[pl.ds(pl.multiple_of((1 - core_ref[0]) * half, half), half), :] = got_ref[...]
        noise = jnp.broadcast_to(g_ref[...], (8, tasks)).T[:, :1]
        for i, s in enumerate(spans):
            reads[i].wait()
            mixed = jnp.dot(f_ref[...], s_buf[:, s], preferred_element_type=jnp.float32)
            o_buf[:, s] = mixed + noise * v_buf[:, s].astype(jnp.float32)
            writes[i].start()
        for copy in writes:
            copy.wait()

    args = [core, own, received, factors, nugget, values]
    specs = [SM, VM, VM, VM, VM, ANY]
    alias = {}
    if product is not None:
        args.append(product)
        specs.append(ANY)
        alias = {6: 0}
    return pl.pallas_call(
        body,
        out_shape=shape(values.shape, jnp.float32),
        in_specs=specs,
        out_specs=ANY,
        scratch_shapes=[
            pltpu.VMEM((tasks, width), values.dtype),
            pltpu.VMEM((tasks, width), jnp.float32),
            pltpu.VMEM((ranks, width), jnp.bfloat16),
            pltpu.SemaphoreType.DMA((steps,)),
            pltpu.SemaphoreType.DMA((steps,)),
        ],
        input_output_aliases=alias,
        compiler_params=grant(10),
        cost_estimate=cost(2 * tasks * ranks * width, tasks * width * 6),
        name="mix",
    )(*args)


def partners(size, bit):
    return [(i, i ^ bit) for i in range(size)]


def sum_fields(share, size):
    bit, other = 2, None
    while bit < size:
        if other is not None:
            share = (share.astype(jnp.float32) + other.astype(jnp.float32)).astype(jnp.bfloat16)
        other = lax.ppermute(share, "task", partners(size, bit))
        bit *= 2
    return share, other


def per_device(values, factors, jitter, length_scales, nugget, neighbours):
    peers, blocks = lax.axis_size("task"), lax.axis_size("site")
    ranks = factors.shape[1]
    lat = length_scales.shape[0] // 2
    rank = ranks // length_scales.shape[0]
    groups = values.shape[1] // GROUP
    core = (lax.axis_index("task") % 2).astype(jnp.int32).reshape(1)
    cuts = [0, groups * 5 // 16, groups * 10 // 16, groups * 14 // 16, groups]
    regions = list(zip(cuts[:-1], cuts[1:]))
    chunk_cuts = [0] + [c + 1 for c in cuts[1:-1]] + [groups]
    chunks = list(zip(chunk_cuts[:-1], chunk_cuts[1:]))

    own, send = project(values, factors, core)
    received = lax.ppermute(send, "task", partners(peers, 1))
    *shares, left_edge, right_edge = add_cores(own, received, jitter, chunks)
    sums = [sum_fields(share, peers) for share in shares]

    up = [(i, (i + 1) % blocks) for i in range(blocks)]
    down = [(j, i) for i, j in up]
    from_left = lax.ppermute(right_edge, "site", up)
    from_right = lax.ppermute(left_edge, "site", down)
    first_half = lax.broadcasted_iota(jnp.int32, from_left.shape, 1) < HALF
    edges = jnp.where(first_half, from_right, from_left)
    edge_sums = sum_fields(edges, peers)

    product = None
    nugget = nugget.reshape(1, -1)
    for n, region in enumerate(regions):
        begin, end = region
        outer = begin == 0 or end == groups
        kernel = kernel_blocks(jitter, edges if outer else None, neighbours, length_scales, core, region, groups, lat)
        pieces = [(*chunks[n], sums[n])]
        if n > 0:
            pieces.append((*chunks[n - 1], sums[n - 1]))
        if begin == 0:
            pieces.append((-1, 0, edge_sums))
        if end == groups:
            pieces.append((groups, groups + 1, edge_sums))
        smoothed = smooth(kernel, region, pieces, lat, rank)
        other = lax.ppermute(smoothed, "task", partners(peers, 1))
        product = mix(smoothed, other, factors, nugget, values, product, core, region)
    return product


def solution(mesh):
    return jax.shard_map(
        per_device,
        mesh=mesh,
        in_specs=(
            P("task", "site"),
            P("task", None),
            P(None, "site"),
            P(),
            P("task"),
            P("site", None),
        ),
        out_specs=P("task", "site"),
        check_vma=False,
    )
```

```python
import jax
import jax.numpy as jnp
from jax import lax
from jax.experimental import pallas as pl
from jax.experimental.pallas import tpu as pltpu
from jax.sharding import PartitionSpec as P


SIDE = 16
GROUP = 128
HALF = GROUP // 2
REACH = 3 * SIDE
KAPPA = 3.0**-0.25
FAR_AWAY = 1024.0
STEP = 512
EDGE_ROWS = 16
MIB = 1 << 20

VM = pl.BlockSpec(memory_space=pltpu.VMEM)
SM = pl.BlockSpec(memory_space=pltpu.SMEM)
HBM = pl.BlockSpec(memory_space=pltpu.HBM)


def shape(dims, kind):
    return jax.ShapeDtypeStruct(dims, kind)


def grant(mib):
    return pltpu.CompilerParams(vmem_limit_bytes=mib * MIB)


def cost(flops, size):
    return pl.CostEstimate(flops=flops, bytes_accessed=size, transcendentals=0)


def project(values, factors, core):
    tasks, ranks = factors.shape
    half, width = ranks // 2, values.shape[1]
    steps = width // STEP

    def body(core_ref, f_hbm, v_hbm, own_ref, send_ref, v_ref, f_ref, sems):
        spans = [pl.ds(i * STEP, STEP) for i in range(steps)]
        first = pltpu.make_async_copy(f_hbm, f_ref, sems.at[steps])
        first.start()
        copies = [pltpu.make_async_copy(v_hbm.at[:, s], v_ref.at[:, s], sems.at[i]) for i, s in enumerate(spans)]
        for copy in copies:
            copy.start()
        is_first = core_ref[0] == 0
        first.wait()
        turned = f_ref[...].astype(jnp.float32).T.astype(jnp.bfloat16)
        for copy, s in zip(copies, spans):
            copy.wait()
            share = jnp.dot(turned, v_ref[:, s], preferred_element_type=jnp.float32)
            own_ref[:, s] = jnp.where(is_first, share[:half], share[half:]).astype(jnp.bfloat16)
            send_ref[:, s] = jnp.where(is_first, share[half:], share[:half]).astype(jnp.bfloat16)

    return pl.pallas_call(
        body,
        out_shape=(
            shape((half, width), jnp.bfloat16),
            shape((half, width), jnp.bfloat16),
        ),
        in_specs=[SM, HBM, HBM],
        out_specs=(VM, VM),
        scratch_shapes=[
            pltpu.VMEM(values.shape, values.dtype),
            pltpu.VMEM(factors.shape, factors.dtype),
            pltpu.SemaphoreType.DMA((steps + 1,)),
        ],
        compiler_params=grant(50),
        cost_estimate=cost(2 * tasks * ranks * width, tasks * width * 2),
        name="project",
    )(core, factors, values)


def add_cores(own, received, jitter, chunks):
    half = own.shape[0]
    edge = half + EDGE_ROWS

    def body(own_ref, got_ref, j_ref, *outs):
        for groups, out in zip(chunks, outs):
            for begin, end in runs(groups):
                s = slice(begin * GROUP, end * GROUP)
                place = groups.index(begin) * GROUP
                total = own_ref[:, s].astype(jnp.float32) + got_ref[:, s].astype(jnp.float32)
                out[:, place : place + (end - begin) * GROUP] = total.astype(jnp.bfloat16)
        for out, s in ((outs[-2], slice(0, GROUP)), (outs[-1], slice(-GROUP, None))):
            out[:half, :] = (own_ref[:, s].astype(jnp.float32) + got_ref[:, s].astype(jnp.float32)).astype(jnp.bfloat16)
            out[half:, :] = jnp.zeros((EDGE_ROWS, GROUP), jnp.bfloat16)
            out[half : half + 2, :] = j_ref[:, s]

    size = [(half, len(groups) * GROUP) for groups in chunks] + [(edge, GROUP)] * 2
    return pl.pallas_call(
        body,
        out_shape=[shape(dims, jnp.bfloat16) for dims in size],
        in_specs=[VM, VM, VM],
        out_specs=[VM] * len(size),
        compiler_params=grant(6),
        cost_estimate=cost(own.size, own.size * 8),
        name="add_cores",
    )(own, received, jitter)


def close_ring(from_left, from_right, share):
    half, width = share.shape

    def body(left_ref, right_ref, share_ref, out, offsets):
        first_half = lax.broadcasted_iota(jnp.int32, (1, GROUP), 1) < HALF
        out[:, :width] = share_ref[...]
        out[:, width:] = jnp.where(first_half, right_ref[:half, :], left_ref[:half, :])
        offsets[...] = jnp.where(first_half, right_ref[half:, :], left_ref[half:, :])

    return pl.pallas_call(
        body,
        out_shape=(shape((half, width + GROUP), share.dtype), shape((EDGE_ROWS, GROUP), share.dtype)),
        in_specs=[VM, VM, VM],
        out_specs=(VM, VM),
        compiler_params=grant(2),
        cost_estimate=cost(share.size, 4 * share.size),
        name="close_ring",
    )(from_left, from_right, share)


def kernel_blocks(jitter, edges, neighbours, scales, core, region, groups, lat):
    rows = GROUP + REACH

    def body(core_ref, near_ref, scale_ref, j_ref, *rest):
        k_ref = rest[-1]
        edge_ref = rest[0]
        lane = lax.broadcasted_iota(jnp.int32, (1, GROUP), 1)
        row, col = ((lane >> 4).astype(jnp.float32), (lane & (SIDE - 1)).astype(jnp.float32))
        corner = lax.broadcasted_iota(jnp.int32, (1, HALF), 1)
        corner_row, corner_col = ((corner >> 4).astype(jnp.float32), (corner & (SIDE - 1)).astype(jnp.float32))
        sub = lax.broadcasted_iota(jnp.int32, (8, GROUP), 0)
        low_half = lax.broadcasted_iota(jnp.int32, (8, GROUP), 1) < HALF
        first_half = lane < HALF
        masks = jnp.where((sub < 3) == low_half, 1.0, 0.0)
        ones = jnp.ones((1, GROUP + HALF), jnp.float32)
        nothing = jnp.zeros((1, GROUP), jnp.float32)
        none = jnp.zeros((8, GROUP), jnp.float32)
        betas = []
        for q in range(lat):
            scale = jnp.full((8, GROUP), scale_ref[core_ref[0] * lat + q], jnp.float32)
            betas.append((1.0 / (KAPPA * scale * scale))[:1])

        def offsets(b):
            if isinstance(b, int):
                return j_ref[:, b * GROUP : (b + 1) * GROUP].astype(jnp.float32)
            return j_ref[:, pl.ds(pl.multiple_of(b * GROUP, GROUP), GROUP)].astype(jnp.float32)

        def block(b, slot):
            here = offsets(b)
            before = edge_ref[:2, :].astype(jnp.float32) if isinstance(b, int) and b == 0 else offsets(b - 1)
            after = edge_ref[:2, :].astype(jnp.float32) if isinstance(b, int) and b == groups - 1 else offsets(b + 1)
            tile, odd = b // 2, b % 2 if isinstance(b, int) else lax.rem(b, 2)
            left_gap = jnp.where((odd == 0) & (near_ref[tile, 1] < 0), FAR_AWAY, 0.0)
            right_gap = jnp.where((odd == 1) & (near_ref[tile, 2] < 0), FAR_AWAY, 0.0)
            far, own = [], []
            for axis, base, end_base in ((0, row, corner_row), (1, col, corner_col)):
                past = pltpu.roll(jnp.broadcast_to(before[axis : axis + 1], (8, GROUP)), REACH, 1)[:1, :HALF]
                gaps = (left_gap, right_gap) if axis == 0 else (0.0, 0.0)
                past_base = end_base - 3.0 if axis == 0 else end_base
                next_base = end_base + 8.0 if axis == 0 else end_base
                far += [
                    jnp.concatenate([here[axis : axis + 1], past], axis=1),
                    jnp.concatenate([base, past_base], axis=1),
                    jnp.concatenate([nothing, jnp.full((1, HALF), gaps[0])], axis=1),
                    jnp.concatenate([here[axis : axis + 1], after[axis : axis + 1, :HALF]], axis=1),
                    jnp.concatenate([base, next_base], axis=1),
                    jnp.concatenate([nothing, jnp.full((1, HALF), gaps[1])], axis=1),
                    ones,
                    ones,
                ]
                mine = jnp.where(sub == 6, -jnp.broadcast_to(here[axis : axis + 1], (8, GROUP)), -jnp.broadcast_to(base, (8, GROUP)))
                own.append(jnp.where(sub < 6, masks, mine))
            left = jnp.concatenate(far, axis=0).T[:rows].astype(jnp.bfloat16)
            right = jnp.concatenate(
                [jnp.concatenate([own[0], none], axis=1), jnp.concatenate([none, own[1]], axis=1)], axis=0
            ).astype(jnp.bfloat16)
            away = jnp.dot(left, right, preferred_element_type=jnp.float32)
            across, sideways = away[:, :GROUP], away[:, GROUP:]
            distance = across * across + sideways * sideways
            for q in range(lat):
                u = jnp.maximum(1.0 / KAPPA - betas[q] * distance, 0.0)
                weight = (u * u * u * (4.0 * KAPPA**3 - u)).astype(jnp.bfloat16)
                s = slice(q * GROUP, (q + 1) * GROUP)
                zero = jnp.zeros((REACH, GROUP), jnp.bfloat16)
                k_ref[slot, :GROUP, s] = weight[:GROUP]
                k_ref[slot, GROUP : GROUP + REACH, s] = jnp.where(first_half, zero, weight[GROUP:])
                k_ref[slot, 2 * GROUP - REACH :, s] = jnp.where(first_half, weight[GROUP:], zero)
            k_ref[slot, GROUP + REACH : 2 * GROUP - REACH, :] = jnp.zeros((GROUP - 2 * REACH, lat * GROUP), jnp.bfloat16)

        count = 4
        for begin, end in runs(region):
            slot = region.index(begin)
            low, high = begin + (begin == 0), end - (end == groups)
            for b in range(begin, low):
                block(b, slot)
            whole = (high - low) // count

            def several(i, carry, low=low, shift=slot - begin):
                for m in range(count):
                    b = low + i * count + m
                    block(b, b + shift)
                return carry

            lax.fori_loop(0, whole, several, 0)
            for b in range(low + whole * count, end):
                block(b, slot + b - begin)

    size = len(region) * 2 * GROUP * lat * GROUP
    args = [core, neighbours, scales, jitter] + ([edges] if edges is not None else [])
    return pl.pallas_call(
        body,
        out_shape=shape((len(region), 2 * GROUP, lat * GROUP), jnp.bfloat16),
        in_specs=[SM, SM, SM] + [VM] * (len(args) - 3),
        out_specs=VM,
        compiler_params=grant(6),
        cost_estimate=cost(30 * size, 2 * size),
        name="kernel_blocks",
    )(*args)


def smooth(blocks, region, pieces, lat, rank, groups):
    half = lat * rank

    def body(k_ref, *refs):
        out = refs[-1]
        first_half = lax.broadcasted_iota(jnp.int32, (1, GROUP), 1) < HALF

        def part(group, which, rows):
            group = groups if group < 0 else group
            for n, (held, _) in enumerate(pieces):
                if group in held:
                    at = held.index(group) * GROUP
                    return refs[2 * n + which][rows, at : at + GROUP]

        for n, b in enumerate(region):
            for q in range(lat):
                rows = slice(q * rank, (q + 1) * rank)
                sides = [
                    jnp.concatenate(
                        [part(b, w, rows), jnp.where(first_half, part(b + 1, w, rows), part(b - 1, w, rows))], axis=1
                    )
                    for w in range(2)
                ]
                total = jnp.dot(
                    jnp.concatenate(sides, axis=0),
                    k_ref[n, :, q * GROUP : (q + 1) * GROUP],
                    preferred_element_type=jnp.float32,
                )
                out[rows, n * GROUP : (n + 1) * GROUP] = (total[:rank] + total[rank:]).astype(jnp.bfloat16)

    arrays = [a for _, pair in pieces for a in pair]
    count = len(region) * GROUP
    return pl.pallas_call(
        body,
        out_shape=shape((half, count), jnp.bfloat16),
        in_specs=[VM] * (1 + len(arrays)),
        out_specs=VM,
        compiler_params=grant(8),
        cost_estimate=cost(8 * half * GROUP * count, 4 * GROUP * lat * count),
        name="smooth",
    )(blocks, *arrays)


def mix(own, received, factors, nugget, values, product, core, region):
    tasks, ranks = factors.shape
    half, width = ranks // 2, len(region) * GROUP
    steps = width // STEP
    places = [region[i * (STEP // GROUP)] * GROUP for i in range(steps)]

    def body(core_ref, own_ref, got_ref, f_ref, g_ref, v_ref, *rest):
        o_hbm, o_buf, s_buf, sems = rest[-4:]
        s_buf[pl.ds(pl.multiple_of(core_ref[0] * half, half), half), :] = own_ref[...]
        s_buf[pl.ds(pl.multiple_of((1 - core_ref[0]) * half, half), half), :] = got_ref[...]
        noise = jnp.broadcast_to(g_ref[...], (8, tasks)).T[:, :1]
        copies = []
        for i, place in enumerate(places):
            s, p = slice(i * STEP, (i + 1) * STEP), slice(place, place + STEP)
            mixed = jnp.dot(f_ref[...], s_buf[:, s], preferred_element_type=jnp.float32)
            o_buf[:, s] = mixed + noise * v_ref[:, p].astype(jnp.float32)
            copies.append(pltpu.make_async_copy(o_buf.at[:, pl.ds(i * STEP, STEP)], o_hbm.at[:, pl.ds(place, STEP)], sems.at[i]))
            copies[-1].start()
        for copy in copies:
            copy.wait()

    args = [core, own, received, factors, nugget, values]
    specs = [SM, VM, VM, VM, VM, VM]
    alias = {}
    if product is not None:
        args.append(product)
        specs.append(HBM)
        alias = {6: 0}
    return pl.pallas_call(
        body,
        out_shape=shape(values.shape, jnp.float32),
        in_specs=specs,
        out_specs=HBM,
        scratch_shapes=[
            pltpu.VMEM((tasks, width), jnp.float32),
            pltpu.VMEM((ranks, width), jnp.bfloat16),
            pltpu.SemaphoreType.DMA((steps,)),
        ],
        input_output_aliases=alias,
        compiler_params=grant(10),
        cost_estimate=cost(2 * tasks * ranks * width, tasks * width * 4),
        name="mix",
    )(*args)


def runs(groups):
    found = []
    for g in groups:
        if found and found[-1][1] == g:
            found[-1][1] = g + 1
        else:
            found.append([g, g + 1])
    return found


def partners(size, bit):
    return [(i, i ^ bit) for i in range(size)]


def sum_fields(share, size):
    bit, other = 2, None
    while bit < size:
        if other is not None:
            share = (share.astype(jnp.float32) + other.astype(jnp.float32)).astype(jnp.bfloat16)
        other = lax.ppermute(share, "task", partners(size, bit))
        bit *= 2
    return share, other


def plan(groups):
    unit = STEP // GROUP
    units = groups // unit
    cuts = [unit * (1 + (units - 2) * n // 14) for n in (0, 5, 10, 14)]
    regions = [list(range(a, b)) for a, b in zip(cuts[:-1], cuts[1:])]
    regions.append(list(range(cuts[-1], groups)) + list(range(cuts[0])))
    starts = [cuts[0] - 1] + [c + 1 for c in cuts[1:]]
    chunks = [list(range(a, b)) for a, b in zip(starts[:-1], starts[1:])]
    chunks.append(list(range(starts[-1], groups)) + list(range(starts[0])))
    return regions, chunks


def steps_of(values, factors, jitter, length_scales, nugget, neighbours):
    peers, blocks = lax.axis_size("task"), lax.axis_size("site")
    ranks = factors.shape[1]
    lat = length_scales.shape[0] // 2
    rank = ranks // length_scales.shape[0]
    groups = values.shape[1] // GROUP
    core = (lax.axis_index("task") % 2).astype(jnp.int32).reshape(1)
    regions, chunks = plan(groups)
    nugget = nugget.reshape(1, -1)

    def build(n):
        edge_offsets = offsets if n == len(regions) - 1 else None
        return kernel_blocks(jitter, edge_offsets, neighbours, length_scales, core, regions[n], groups, lat)

    own, send = project(values, factors, core)
    received = lax.ppermute(send, "task", partners(peers, 1))
    *shares, left_edge, right_edge = add_cores(own, received, jitter, chunks)
    sums = []
    for share in shares[:-1]:
        sums.append(sum_fields(share, peers))
    up = [(i, (i + 1) % blocks) for i in range(blocks)]
    down = [(j, i) for i, j in up]
    from_left = lax.ppermute(right_edge, "site", up)
    from_right = lax.ppermute(left_edge, "site", down)
    last, offsets = close_ring(from_left, from_right, shares[-1])
    sums.append(sum_fields(last, peers))
    held_groups = chunks[:-1] + [chunks[-1] + [groups]]

    product = None
    for n, region in enumerate(regions):
        kernel = build(n)
        pieces = [(held_groups[n], sums[n])]
        if n > 0:
            pieces.append((held_groups[n - 1], sums[n - 1]))
        if n == len(regions) - 1:
            pieces.append((held_groups[0], sums[0]))
        smoothed = smooth(kernel, region, pieces, lat, rank, groups)
        other = lax.ppermute(smoothed, "task", partners(peers, 1))
        product = mix(smoothed, other, factors, nugget, values, product, core, region)
    return product


def solution(mesh):
    return jax.shard_map(
        steps_of,
        mesh=mesh,
        in_specs=(
            P("task", "site"),
            P("task", None),
            P(None, "site"),
            P(),
            P("task"),
            P("site", None),
        ),
        out_specs=P("task", "site"),
        check_vma=False,
    )
```

```python
import jax
import jax.numpy as jnp
from jax import lax
from jax.experimental import pallas as pl
from jax.experimental.pallas import tpu as pltpu
from jax.sharding import PartitionSpec as P


SIDE = 16
GROUP = 128
HALF = GROUP // 2
REACH = 3 * SIDE
KAPPA = 3.0**-0.25
FAR_AWAY = 1024.0
STEP = 512
EDGE_ROWS = 16
MIB = 1 << 20
CUTS = (5, 11)
ROOMS = (10, 14)

VM = pl.BlockSpec(memory_space=pltpu.VMEM)
HBM = pl.BlockSpec(memory_space=pltpu.HBM)


def shape(dims, kind):
    return jax.ShapeDtypeStruct(dims, kind)


def in_hbm(x):
    return pltpu.with_memory_space_constraint(x, pltpu.HBM)


def grant(mib):
    return pltpu.CompilerParams(vmem_limit_bytes=mib * MIB)


def cost(flops, size):
    return pl.CostEstimate(flops=flops, bytes_accessed=size, transcendentals=0)


def tiles(groups):
    found, place = [], 0
    for begin, end in runs(groups):
        for at in range(begin * GROUP, end * GROUP, STEP):
            size = min(STEP, end * GROUP - at)
            found.append((at, place, size))
            place += size
    return found


def project(values, factors, groups, small=None, room=50):
    tasks, ranks = factors.shape
    half, width = ranks // 2, len(groups) * GROUP
    cuts = tiles(groups)

    def body(*refs):
        count = 2 + (3 if small else 0)
        f_hbm, v_hbm = refs[:2]
        own_ref, send_ref = refs[count : count + 2]
        v_ref, f_ref, sems = refs[-3:]
        first = pltpu.make_async_copy(f_hbm, f_ref, sems.at[len(cuts)])
        first.start()
        copies = [
            pltpu.make_async_copy(v_hbm.at[:, pl.ds(at, size)], v_ref.at[:, pl.ds(place, size)], sems.at[i])
            for i, (at, place, size) in enumerate(cuts)
        ]
        for copy in copies:
            copy.start()
        core = lax.rem(lax.axis_index("task"), 2)
        if small:
            j_hbm, n_hbm, s_hbm = refs[2:5]
            j_out, gap_out, beta_out, n_ref, s_ref, extra = refs[count + 2 : count + 8]
            others = [
                pltpu.make_async_copy(x, y, extra.at[i])
                for i, (x, y) in enumerate(((j_hbm, j_out), (n_hbm, n_ref), (s_hbm, s_ref)))
            ]
            for copy in others:
                copy.start()
        first.wait()
        turned = f_ref[...].astype(jnp.float32).T.astype(jnp.bfloat16)
        for copy, (_, place, size) in zip(copies, cuts):
            copy.wait()
            s = slice(place, place + size)
            share = jnp.dot(turned, v_ref[:, s], preferred_element_type=jnp.float32)
            own_ref[:, s] = jnp.where(core == 0, share[:half], share[half:])
            send_ref[:, s] = jnp.where(core == 0, share[half:], share[:half]).astype(jnp.bfloat16)
        if small:
            for copy in others:
                copy.wait()
            owner = n_ref.shape[1]
            lane = lax.broadcasted_iota(jnp.int32, (owner, GROUP), 1)
            for parity in range(2):
                cut = jnp.where(n_ref[parity + 1 : parity + 2, :] < 0, FAR_AWAY, 0.0)
                column = jnp.broadcast_to(cut, (8, owner)).T[:, :1]
                gap_out[parity] = jnp.where((lane < HALF) == (parity == 0), jnp.broadcast_to(column, (owner, GROUP)), 0.0)
            count_q = s_ref.shape[1]
            lat = count_q // 2
            scale = s_ref[...]
            which = lax.broadcasted_iota(jnp.int32, (1, count_q), 1)
            beta = 1.0 / (KAPPA * scale * scale)
            for q in range(lat):
                value = jnp.sum(jnp.where(which == core * lat + q, beta, 0.0), axis=1, keepdims=True)
                beta_out[8 * q : 8 * q + 8, :] = jnp.broadcast_to(value, (8, GROUP))

    out = [shape((half, width), jnp.float32), shape((half, width), jnp.bfloat16)]
    scratch = []
    if small:
        offsets, near, scales = small
        lat = scales.shape[1] // 2
        out += [
            shape(offsets.shape, offsets.dtype),
            shape((2, near.shape[1], GROUP), jnp.float32),
            shape((8 * lat, GROUP), jnp.float32),
        ]
        scratch = [pltpu.VMEM(near.shape, near.dtype), pltpu.VMEM(scales.shape, scales.dtype), pltpu.SemaphoreType.DMA((3,))]
    args = [in_hbm(x) for x in (factors, values, *(small or ()))]
    return pl.pallas_call(
        body,
        out_shape=out,
        in_specs=[HBM] * len(args),
        out_specs=[VM] * len(out),
        scratch_shapes=scratch
        + [
            pltpu.VMEM((tasks, width), values.dtype),
            pltpu.VMEM(factors.shape, factors.dtype),
            pltpu.SemaphoreType.DMA((len(cuts) + 1,)),
        ],
        compiler_params=pltpu.CompilerParams(vmem_limit_bytes=int(room * MIB)),
        cost_estimate=cost(2 * tasks * ranks * width, tasks * width * 2),
        name="project",
    )(*args)


def add_cores(own, received, held, chunks, offsets=None):
    half = own.shape[0]
    edge = half + EDGE_ROWS

    def body(own_ref, got_ref, *refs):
        outs = refs[(0 if offsets is None else 1) :]

        def total(begin, end):
            s = slice(held.index(begin) * GROUP, held.index(end - 1) * GROUP + GROUP)
            return (own_ref[:, s] + got_ref[:, s].astype(jnp.float32)).astype(jnp.bfloat16)

        for groups, out in zip(chunks, outs):
            for begin, end in runs(groups):
                place = groups.index(begin) * GROUP
                out[:, place : place + (end - begin) * GROUP] = total(begin, end)
        if offsets is not None:
            last = offsets.shape[1] // GROUP - 1
            for out, g in ((outs[-2], 0), (outs[-1], last)):
                out[:half, :] = total(g, g + 1)
                out[half:, :] = jnp.zeros((EDGE_ROWS, GROUP), jnp.bfloat16)
                out[half : half + 2, :] = refs[0][:, g * GROUP : (g + 1) * GROUP]

    size = [(half, len(groups) * GROUP) for groups in chunks]
    args = [own, received]
    if offsets is not None:
        size += [(edge, GROUP)] * 2
        args.append(offsets)
    return pl.pallas_call(
        body,
        out_shape=[shape(dims, jnp.bfloat16) for dims in size],
        in_specs=[VM] * len(args),
        out_specs=[VM] * len(size),
        compiler_params=grant(6),
        cost_estimate=cost(own.size, own.size * 6),
        name="add_cores",
    )(*args)


def close_ring(from_left, from_right, share):
    half, width = share.shape

    def body(left_ref, right_ref, share_ref, out, offsets):
        first_half = lax.broadcasted_iota(jnp.int32, (1, GROUP), 1) < HALF
        out[:, :width] = share_ref[...]
        out[:, width:] = jnp.where(first_half, right_ref[:half, :], left_ref[:half, :])
        offsets[...] = jnp.where(first_half, right_ref[half:, :], left_ref[half:, :])

    return pl.pallas_call(
        body,
        out_shape=(shape((half, width + GROUP), share.dtype), shape((EDGE_ROWS, GROUP), share.dtype)),
        in_specs=[VM, VM, VM],
        out_specs=(VM, VM),
        compiler_params=grant(2),
        cost_estimate=cost(share.size, 4 * share.size),
        name="close_ring",
    )(from_left, from_right, share)


def kernel_blocks(offsets, gaps, betas, edges, region, groups):
    lat = betas.shape[0] // 8
    rows = GROUP + REACH
    wide = 2 * GROUP

    def body(j_ref, gap_ref, beta_ref, *rest):
        k_ref = rest[-1]
        edge_ref = rest[0]
        sub = lax.broadcasted_iota(jnp.int32, (8, wide), 0)
        lane = lax.broadcasted_iota(jnp.int32, (8, wide), 1)
        row, col = ((lane >> 4).astype(jnp.float32), (lane & (SIDE - 1)).astype(jnp.float32))
        corner = lane >= GROUP
        past_row = jnp.where(corner, row - 11.0, row)
        zero = jnp.zeros_like(row)
        far_base = (
            jnp.where(sub == 1, past_row, jnp.where(sub == 4, row, jnp.where(sub >= 6, 1.0, zero))),
            jnp.where((sub == 1) | (sub == 4), col, jnp.where(sub >= 6, 1.0, zero)),
        )
        sub_1, lane_1 = sub[:, :GROUP], lane[:, :GROUP]
        meets = jnp.where((sub_1 < 3) == (lane_1 < HALF), 1.0, 0.0)
        own_base = tuple(jnp.where(sub_1 < 6, meets, -base[:, :GROUP]) for base in (row, col))
        none = jnp.zeros((8, GROUP), jnp.float32)
        first_half = lax.broadcasted_iota(jnp.int32, (1, GROUP), 1) < HALF
        scale = [beta_ref[8 * q : 8 * q + 1, :] for q in range(lat)]

        def columns(b):
            if isinstance(b, int):
                return j_ref[:, b * GROUP : (b + 1) * GROUP].astype(jnp.float32)
            return j_ref[:, pl.ds(pl.multiple_of(b * GROUP, GROUP), GROUP)].astype(jnp.float32)

        def eight(x):
            return jnp.broadcast_to(x, (8, GROUP))

        def block(b, parity, slot):
            here = columns(b)
            before = edge_ref[:2, :].astype(jnp.float32) if isinstance(b, int) and b == 0 else columns(b - 1)
            after = edge_ref[:2, :].astype(jnp.float32) if isinstance(b, int) and b == groups - 1 else columns(b + 1)
            gap = eight(gap_ref[parity, pl.ds(b // 2, 1), :])
            far, own = [], []
            for axis in range(2):
                mine = eight(here[axis : axis + 1])
                past = pltpu.roll(eight(before[axis : axis + 1]), REACH, 1)
                coming = eight(after[axis : axis + 1])
                base = far_base[axis]
                left = jnp.where((sub_1 == 0) | (sub_1 == 3), mine, base[:, :GROUP])
                right = jnp.where(sub_1 == 0, past, jnp.where(sub_1 == 3, coming, base[:, GROUP:]))
                if axis == 0 and parity == 0:
                    right = jnp.where(sub_1 == 2, gap, right)
                if axis == 0 and parity == 1:
                    right = jnp.where(sub_1 == 5, pltpu.roll(gap, HALF, 1), right)
                far.append(jnp.concatenate([left, right], axis=1))
                own.append(jnp.where(sub_1 == 6, -mine, own_base[axis]))
            left = jnp.concatenate(far, axis=0).T[:rows].astype(jnp.bfloat16)
            right = jnp.concatenate(
                [jnp.concatenate([own[0], none], axis=1), jnp.concatenate([none, own[1]], axis=1)], axis=0
            ).astype(jnp.bfloat16)
            away = jnp.dot(left, right, preferred_element_type=jnp.float32)
            across, sideways = away[:, :GROUP], away[:, GROUP:]
            distance = across * across + sideways * sideways
            for q in range(lat):
                u = jnp.maximum(1.0 / KAPPA - scale[q] * distance, 0.0)
                weight = (u * u * u * (4.0 * KAPPA**3 - u)).astype(jnp.bfloat16)
                s = slice(q * GROUP, (q + 1) * GROUP)
                blank = jnp.zeros((REACH, GROUP), jnp.bfloat16)
                k_ref[slot, :GROUP, s] = weight[:GROUP]
                k_ref[slot, GROUP : GROUP + REACH, s] = jnp.where(first_half, blank, weight[GROUP:])
                k_ref[slot, wide - REACH :, s] = jnp.where(first_half, weight[GROUP:], blank)
            k_ref[slot, GROUP + REACH : wide - REACH, :] = jnp.zeros((GROUP - 2 * REACH, lat * GROUP), jnp.bfloat16)

        count = 8
        for begin, end in runs(region):
            slot = region.index(begin)
            low, high = begin + (begin == 0), end - (end == groups)
            low += low % 2
            for b in range(begin, low):
                block(b, b % 2, slot + b - begin)
            whole = (high - low) // count

            def several(i, carry, low=low, shift=slot - begin):
                for m in range(count):
                    b = low + i * count + m
                    block(b, m % 2, b + shift)
                return carry

            if whole > 1:
                lax.fori_loop(0, whole, several, 0)
            else:
                whole = 0
            for b in range(low + whole * count, end):
                block(b, b % 2, slot + b - begin)

    size = len(region) * wide * lat * GROUP
    args = [offsets, gaps, betas] + ([edges] if edges is not None else [])
    return pl.pallas_call(
        body,
        out_shape=shape((len(region), wide, lat * GROUP), jnp.bfloat16),
        in_specs=[VM] * len(args),
        out_specs=VM,
        compiler_params=grant(6),
        cost_estimate=cost(30 * size, 2 * size),
        name="kernel_blocks",
    )(*args)


def smooth(blocks, region, pieces, lat, rank, groups):
    half = lat * rank

    def body(k_ref, *refs):
        out = refs[-1]
        first_half = lax.broadcasted_iota(jnp.int32, (1, GROUP), 1) < HALF

        def part(group, which, rows):
            group = groups if group < 0 else group
            for n, (held, _) in enumerate(pieces):
                if group in held:
                    at = held.index(group) * GROUP
                    return refs[2 * n + which][rows, at : at + GROUP]

        for n, b in enumerate(region):
            for q in range(lat):
                rows = slice(q * rank, (q + 1) * rank)
                sides = [
                    jnp.concatenate(
                        [part(b, w, rows), jnp.where(first_half, part(b + 1, w, rows), part(b - 1, w, rows))], axis=1
                    )
                    for w in range(2)
                ]
                total = jnp.dot(
                    jnp.concatenate(sides, axis=0),
                    k_ref[n, :, q * GROUP : (q + 1) * GROUP],
                    preferred_element_type=jnp.float32,
                )
                out[rows, n * GROUP : (n + 1) * GROUP] = (total[:rank] + total[rank:]).astype(jnp.bfloat16)

    arrays = [a for _, pair in pieces for a in pair]
    count = len(region) * GROUP
    return pl.pallas_call(
        body,
        out_shape=shape((half, count), jnp.bfloat16),
        in_specs=[VM] * (1 + len(arrays)),
        out_specs=VM,
        compiler_params=grant(8),
        cost_estimate=cost(8 * half * GROUP * count, 4 * GROUP * lat * count),
        name="smooth",
    )(blocks, *arrays)


def mix(own, received, factors, nugget, values, product, region):
    tasks, ranks = factors.shape
    half, width = ranks // 2, len(region) * GROUP
    steps = width // STEP
    places = [region[i * (STEP // GROUP)] * GROUP for i in range(steps)]

    def body(own_ref, got_ref, f_ref, g_ref, v_ref, *rest):
        o_hbm, o_buf, s_buf, sems = rest[-4:]
        core = lax.rem(lax.axis_index("task"), 2)
        s_buf[pl.ds(pl.multiple_of(core * half, half), half), :] = own_ref[...]
        s_buf[pl.ds(pl.multiple_of((1 - core) * half, half), half), :] = got_ref[...]
        noise = jnp.broadcast_to(g_ref[...], (8, tasks)).T[:, :1]
        copies = []
        for i, place in enumerate(places):
            s, p = slice(i * STEP, (i + 1) * STEP), slice(place, place + STEP)
            mixed = jnp.dot(f_ref[...], s_buf[:, s], preferred_element_type=jnp.float32)
            o_buf[:, s] = mixed + noise * v_ref[:, p].astype(jnp.float32)
            copies.append(pltpu.make_async_copy(o_buf.at[:, pl.ds(i * STEP, STEP)], o_hbm.at[:, pl.ds(place, STEP)], sems.at[i]))
            copies[-1].start()
        for copy in copies:
            copy.wait()

    args = [own, received, factors, nugget, values]
    specs = [VM, VM, VM, VM, VM]
    alias = {}
    if product is not None:
        args.append(product)
        specs.append(HBM)
        alias = {5: 0}
    return pl.pallas_call(
        body,
        out_shape=shape(values.shape, jnp.float32),
        in_specs=specs,
        out_specs=HBM,
        scratch_shapes=[
            pltpu.VMEM((tasks, width), jnp.float32),
            pltpu.VMEM((ranks, width), jnp.bfloat16),
            pltpu.SemaphoreType.DMA((steps,)),
        ],
        input_output_aliases=alias,
        compiler_params=grant(10),
        cost_estimate=cost(2 * tasks * ranks * width, tasks * width * 4),
        name="mix",
    )(*args)


def runs(groups):
    found = []
    for g in groups:
        if found and found[-1][1] == g:
            found[-1][1] = g + 1
        else:
            found.append([g, g + 1])
    return found


def partners(size, bit):
    return [(i, i ^ bit) for i in range(size)]


def sum_fields(share, size):
    bit, other = 2, None
    while bit < size:
        if other is not None:
            share = (share.astype(jnp.float32) + other.astype(jnp.float32)).astype(jnp.bfloat16)
        other = lax.ppermute(share, "task", partners(size, bit))
        bit *= 2
    return share, other


def plan(groups):
    unit = STEP // GROUP
    units = groups // unit
    cuts = [unit * (1 + (units - 2) * n // 14) for n in (0, *CUTS)]
    regions = [list(range(a, b)) for a, b in zip(cuts[:-1], cuts[1:])]
    regions.append(list(range(cuts[-1], groups)) + list(range(cuts[0])))
    starts = [cuts[0] - 1] + [c + 1 for c in cuts[1:]]
    chunks = [list(range(a, b)) for a, b in zip(starts[:-1], starts[1:])]
    chunks.append(list(range(starts[-1], groups)) + list(range(starts[0])))
    return regions, chunks


def steps_of(values, factors, jitter, length_scales, nugget, neighbours):
    peers, blocks = lax.axis_size("task"), lax.axis_size("site")
    ranks = factors.shape[1]
    lat = length_scales.shape[0] // 2
    rank = ranks // length_scales.shape[0]
    groups = values.shape[1] // GROUP
    regions, chunks = plan(groups)
    nugget = nugget.reshape(1, -1)
    small = (jitter, neighbours.T, length_scales.reshape(1, -1))

    def build(n):
        edge_offsets = outside if n == len(regions) - 1 else None
        return kernel_blocks(offsets, gaps, betas, edge_offsets, regions[n], groups)

    rest = [g for chunk in chunks[1:] for g in chunk]
    own, send, offsets, gaps, betas = project(values, factors, chunks[0], small, room=ROOMS[0])
    received = lax.ppermute(send, "task", partners(peers, 1))
    (share,) = add_cores(own, received, chunks[0], chunks[:1])
    sums = [sum_fields(share, peers)]
    own, send = project(values, factors, rest, room=ROOMS[1])
    received = lax.ppermute(send, "task", partners(peers, 1))
    *shares, left_edge, right_edge = add_cores(own, received, rest, chunks[1:], offsets)
    for share in shares[:-1]:
        sums.append(sum_fields(share, peers))
    up = [(i, (i + 1) % blocks) for i in range(blocks)]
    down = [(j, i) for i, j in up]
    from_left = lax.ppermute(right_edge, "site", up)
    from_right = lax.ppermute(left_edge, "site", down)
    last, outside = close_ring(from_left, from_right, shares[-1])
    sums.append(sum_fields(last, peers))
    held_groups = chunks[:-1] + [chunks[-1] + [groups]]

    product = None
    for n, region in enumerate(regions):
        kernel = build(n)
        pieces = [(held_groups[n], sums[n])]
        if n > 0:
            pieces.append((held_groups[n - 1], sums[n - 1]))
        if n == len(regions) - 1:
            pieces.append((held_groups[0], sums[0]))
        smoothed = smooth(kernel, region, pieces, lat, rank, groups)
        other = lax.ppermute(smoothed, "task", partners(peers, 1))
        product = mix(smoothed, other, factors, nugget, values, product, region)
    return product


def solution(mesh):
    return jax.shard_map(
        steps_of,
        mesh=mesh,
        in_specs=(
            P("task", "site"),
            P("task", None),
            P(None, "site"),
            P(),
            P("task"),
            P("site", None),
        ),
        out_specs=P("task", "site"),
        check_vma=False,
    )
```

```python
import jax
import jax.numpy as jnp
from jax import lax
from jax.experimental import pallas as pl
from jax.experimental.pallas import tpu as pltpu
from jax.sharding import PartitionSpec as P


SIDE = 16
GROUP = 128
HALF = GROUP // 2
REACH = 3 * SIDE
KAPPA = 3.0**-0.25
FAR_AWAY = 1024.0
STEP = 512
EDGE_ROWS = 16
MIB = 1 << 20
CUTS = (9, 22, 28)

VM = pl.BlockSpec(memory_space=pltpu.VMEM)
HBM = pl.BlockSpec(memory_space=pltpu.HBM)


def shape(dims, kind):
    return jax.ShapeDtypeStruct(dims, kind)


def in_hbm(x):
    return pltpu.with_memory_space_constraint(x, pltpu.HBM)


def grant(mib):
    return pltpu.CompilerParams(vmem_limit_bytes=mib * MIB)


def cost(flops, size):
    return pl.CostEstimate(flops=flops, bytes_accessed=size, transcendentals=0)


def tiles(groups):
    found, place = [], 0
    for begin, end in runs(groups):
        for at in range(begin * GROUP, end * GROUP, STEP):
            size = min(STEP, end * GROUP - at)
            found.append((at, place, size))
            place += size
    return found


def core_of():
    return lax.rem(lax.axis_index("task"), 2)


def columns(begin, size, side, span):
    return pl.ds(pl.multiple_of(side * span + begin, GROUP), size)


def project(values, factors, groups, resident):
    tasks, ranks = factors.shape
    span, width = values.shape[1] // 2, len(groups) * GROUP
    cuts = tiles(groups)

    def body(f_hbm, v_hbm, own_ref, send_ref, v_ref, f_ref, sems):
        core = core_of()
        first = pltpu.make_async_copy(f_hbm, f_ref, sems.at[2 * len(cuts)])
        first.start()
        work = [(send_ref, 1 - core, *cut) for cut in cuts] + [(own_ref, core, *cut) for cut in cuts]
        copies = [] if resident else [
            pltpu.make_async_copy(v_hbm.at[:, columns(at, size, side, span)], v_ref.at[i // len(cuts), :, pl.ds(place, size)], sems.at[i])
            for i, (_, side, at, place, size) in enumerate(work)
        ]
        for copy in copies:
            copy.start()
        first.wait()
        turned = f_ref[...].astype(jnp.float32).T.astype(jnp.bfloat16)
        for i, (out, side, at, place, size) in enumerate(work):
            s = slice(place, place + size)
            if resident:
                field = v_hbm[:, columns(at, size, side, span)]
            else:
                copies[i].wait()
                field = v_ref[i // len(cuts), :, s]
            out[:, s] = jnp.dot(turned, field, preferred_element_type=jnp.float32).astype(out.dtype)

    return pl.pallas_call(
        body,
        out_shape=(shape((ranks, width), jnp.float32), shape((ranks, width), jnp.bfloat16)),
        in_specs=[HBM, VM if resident else HBM],
        out_specs=(VM, VM),
        scratch_shapes=[
            pltpu.VMEM((1, 16, GROUP) if resident else (2, tasks, width), values.dtype),
            pltpu.VMEM(factors.shape, factors.dtype),
            pltpu.SemaphoreType.DMA((2 * len(cuts) + 1,)),
        ],
        compiler_params=grant(14),
        cost_estimate=cost(4 * tasks * ranks * width, tasks * width * 4),
        name="project",
    )(in_hbm(factors), values if resident else in_hbm(values))


def make_tables(jitter, neighbours, scales):
    span, owner, lat = jitter.shape[1] // 2, neighbours.shape[1], scales.shape[1]

    def body(j_hbm, n_hbm, s_hbm, j_out, gap_out, beta_out, n_ref, s_ref, gap_ref, sems):
        core = core_of()
        copies = [
            pltpu.make_async_copy(j_hbm.at[:, columns(0, span, core, span)], j_out, sems.at[0]),
            pltpu.make_async_copy(n_hbm, n_ref, sems.at[1]),
            pltpu.make_async_copy(s_hbm, s_ref, sems.at[2]),
        ]
        for copy in copies:
            copy.start()
        for copy in copies:
            copy.wait()
        lane = lax.broadcasted_iota(jnp.int32, (owner, GROUP), 1)
        for parity in range(2):
            cut = jnp.where(n_ref[parity + 1 : parity + 2, :] < 0, FAR_AWAY, 0.0)
            column = jnp.broadcast_to(cut, (8, owner)).T[:, :1]
            gap_ref[parity] = jnp.where((lane < HALF) == (parity == 0), jnp.broadcast_to(column, (owner, GROUP)), 0.0)
            mine = pl.multiple_of(core * (owner // 2), owner // 2)
            gap_out[parity] = gap_ref[parity, pl.ds(mine, owner // 2), :]
        scale = s_ref[...]
        which = lax.broadcasted_iota(jnp.int32, scale.shape, 1)
        beta = 1.0 / (KAPPA * scale * scale)
        for q in range(lat):
            value = jnp.sum(jnp.where(which == q, beta, 0.0), axis=1, keepdims=True)
            beta_out[8 * q : 8 * q + 8, :] = jnp.broadcast_to(value, (8, GROUP))

    return pl.pallas_call(
        body,
        out_shape=(
            shape((2, span), jitter.dtype),
            shape((2, owner // 2, GROUP), jnp.float32),
            shape((8 * lat, GROUP), jnp.float32),
        ),
        in_specs=[HBM] * 3,
        out_specs=(VM, VM, VM),
        scratch_shapes=[
            pltpu.VMEM(neighbours.shape, neighbours.dtype),
            pltpu.VMEM(scales.shape, scales.dtype),
            pltpu.VMEM((2, owner, GROUP), jnp.float32),
            pltpu.SemaphoreType.DMA((3,)),
        ],
        compiler_params=grant(2),
        cost_estimate=cost(jitter.size, 4 * jitter.size),
        name="make_tables",
    )(in_hbm(jitter), in_hbm(neighbours), in_hbm(scales))


def add_cores(own, received, held, chunks):
    ranks = own.shape[0]

    def body(own_ref, got_ref, *outs):
        for groups, out in zip(chunks, outs):
            for begin, end in runs(groups):
                place = groups.index(begin) * GROUP
                s = slice(held.index(begin) * GROUP, held.index(end - 1) * GROUP + GROUP)
                total = own_ref[:, s] + got_ref[:, s].astype(jnp.float32)
                out[:, place : place + (end - begin) * GROUP] = total.astype(jnp.bfloat16)

    return pl.pallas_call(
        body,
        out_shape=[shape((ranks, len(groups) * GROUP), jnp.bfloat16) for groups in chunks],
        in_specs=[VM, VM],
        out_specs=[VM] * len(chunks),
        compiler_params=grant(8),
        cost_estimate=cost(own.size, own.size * 6),
        name="add_cores",
    )(own, received)


def take_edges(first, last, offsets):
    ranks = first.shape[0]

    def body(first_ref, last_ref, j_ref, *outs):
        for out, source, s in ((outs[0], first_ref, slice(0, GROUP)), (outs[1], last_ref, slice(-GROUP, None))):
            out[:ranks, :] = source[:, s]
            out[ranks:, :] = jnp.zeros((EDGE_ROWS, GROUP), jnp.bfloat16)
            out[ranks : ranks + 2, :] = j_ref[:, s]

    return pl.pallas_call(
        body,
        out_shape=[shape((ranks + EDGE_ROWS, GROUP), jnp.bfloat16)] * 2,
        in_specs=[VM] * 3,
        out_specs=[VM] * 2,
        compiler_params=grant(3),
        cost_estimate=cost(first.size, first.size),
        name="take_edges",
    )(first, last, offsets)


def close_ring(from_left, from_right, share):
    half, width = share.shape

    def body(left_ref, right_ref, share_ref, out, offsets):
        first_half = lax.broadcasted_iota(jnp.int32, (1, GROUP), 1) < HALF
        out[:, :width] = share_ref[...]
        out[:, width:] = jnp.where(first_half, right_ref[:half, :], left_ref[:half, :])
        offsets[...] = jnp.where(first_half, right_ref[half:, :], left_ref[half:, :])

    return pl.pallas_call(
        body,
        out_shape=(shape((half, width + GROUP), share.dtype), shape((EDGE_ROWS, GROUP), share.dtype)),
        in_specs=[VM, VM, VM],
        out_specs=(VM, VM),
        compiler_params=grant(2),
        cost_estimate=cost(share.size, 4 * share.size),
        name="close_ring",
    )(from_left, from_right, share)


def kernel_blocks(offsets, gaps, betas, edges, region, groups):
    lat = betas.shape[0] // 8
    rows = GROUP + REACH
    wide = 2 * GROUP

    def body(j_ref, gap_ref, beta_ref, *rest):
        k_ref = rest[-1]
        edge_ref = rest[0]
        sub = lax.broadcasted_iota(jnp.int32, (8, wide), 0)
        lane = lax.broadcasted_iota(jnp.int32, (8, wide), 1)
        row, col = ((lane >> 4).astype(jnp.float32), (lane & (SIDE - 1)).astype(jnp.float32))
        corner = lane >= GROUP
        past_row = jnp.where(corner, row - 11.0, row)
        zero = jnp.zeros_like(row)
        far_base = (
            jnp.where(sub == 1, past_row, jnp.where(sub == 4, row, jnp.where(sub >= 6, 1.0, zero))),
            jnp.where((sub == 1) | (sub == 4), col, jnp.where(sub >= 6, 1.0, zero)),
        )
        sub_1, lane_1 = sub[:, :GROUP], lane[:, :GROUP]
        meets = jnp.where((sub_1 < 3) == (lane_1 < HALF), 1.0, 0.0)
        own_base = tuple(jnp.where(sub_1 < 6, meets, -base[:, :GROUP]) for base in (row, col))
        none = jnp.zeros((8, GROUP), jnp.float32)
        first_half = lax.broadcasted_iota(jnp.int32, (1, GROUP), 1) < HALF
        scale = [beta_ref[8 * q : 8 * q + 1, :] for q in range(lat)]

        def offsets_of(b):
            if isinstance(b, int):
                return j_ref[:, b * GROUP : (b + 1) * GROUP].astype(jnp.float32)
            return j_ref[:, pl.ds(pl.multiple_of(b * GROUP, GROUP), GROUP)].astype(jnp.float32)

        def eight(x):
            return jnp.broadcast_to(x, (8, GROUP))

        def block(b, parity, slot):
            here = offsets_of(b)
            before = edge_ref[:2, :].astype(jnp.float32) if isinstance(b, int) and b == 0 else offsets_of(b - 1)
            after = edge_ref[:2, :].astype(jnp.float32) if isinstance(b, int) and b == groups - 1 else offsets_of(b + 1)
            gap = eight(gap_ref[parity, pl.ds(b // 2, 1), :])
            far, own = [], []
            for axis in range(2):
                mine = eight(here[axis : axis + 1])
                past = pltpu.roll(eight(before[axis : axis + 1]), REACH, 1)
                coming = eight(after[axis : axis + 1])
                base = far_base[axis]
                left = jnp.where((sub_1 == 0) | (sub_1 == 3), mine, base[:, :GROUP])
                right = jnp.where(sub_1 == 0, past, jnp.where(sub_1 == 3, coming, base[:, GROUP:]))
                if axis == 0 and parity == 0:
                    right = jnp.where(sub_1 == 2, gap, right)
                if axis == 0 and parity == 1:
                    right = jnp.where(sub_1 == 5, pltpu.roll(gap, HALF, 1), right)
                far.append(jnp.concatenate([left, right], axis=1))
                own.append(jnp.where(sub_1 == 6, -mine, own_base[axis]))
            left = jnp.concatenate(far, axis=0).T[:rows].astype(jnp.bfloat16)
            right = jnp.concatenate(
                [jnp.concatenate([own[0], none], axis=1), jnp.concatenate([none, own[1]], axis=1)], axis=0
            ).astype(jnp.bfloat16)
            away = jnp.dot(left, right, preferred_element_type=jnp.float32)
            across, sideways = away[:, :GROUP], away[:, GROUP:]
            distance = across * across + sideways * sideways
            for q in range(lat):
                u = jnp.maximum(1.0 / KAPPA - scale[q] * distance, 0.0)
                weight = (u * u * u * (4.0 * KAPPA**3 - u)).astype(jnp.bfloat16)
                s = slice(q * GROUP, (q + 1) * GROUP)
                blank = jnp.zeros((REACH, GROUP), jnp.bfloat16)
                k_ref[slot, :GROUP, s] = weight[:GROUP]
                k_ref[slot, GROUP : GROUP + REACH, s] = jnp.where(first_half, blank, weight[GROUP:])
                k_ref[slot, wide - REACH :, s] = jnp.where(first_half, weight[GROUP:], blank)
            k_ref[slot, GROUP + REACH : wide - REACH, :] = jnp.zeros((GROUP - 2 * REACH, lat * GROUP), jnp.bfloat16)

        count = 4
        for begin, end in runs(region):
            slot = region.index(begin)
            low, high = begin + (begin == 0), end - (end == groups)
            low = min(low + low % 2, end)
            for b in range(begin, low):
                block(b, b % 2, slot + b - begin)
            whole = (high - low) // count

            def several(i, carry, low=low, shift=slot - begin):
                for m in range(count):
                    b = low + i * count + m
                    block(b, m % 2, b + shift)
                return carry

            if whole > 1:
                lax.fori_loop(0, whole, several, 0)
            else:
                whole = 0
            for b in range(low + whole * count, end):
                block(b, b % 2, slot + b - begin)

    size = len(region) * wide * lat * GROUP
    args = [offsets, gaps, betas] + ([edges] if edges is not None else [])
    return pl.pallas_call(
        body,
        out_shape=shape((len(region), wide, lat * GROUP), jnp.bfloat16),
        in_specs=[VM] * len(args),
        out_specs=VM,
        compiler_params=grant(6),
        cost_estimate=cost(30 * size, 2 * size),
        name="kernel_blocks",
    )(*args)


def smooth(kernels, region, pieces, lat, rank, groups):
    half = lat * rank
    owners = [(k, m) for k, kernel in enumerate(kernels) for m in range(kernel.shape[0])]

    def body(*refs):
        k_refs, refs = refs[: len(kernels)], refs[len(kernels) :]
        out = refs[-1]
        first_half = lax.broadcasted_iota(jnp.int32, (1, GROUP), 1) < HALF

        def part(group, which, rows):
            group = groups if group < 0 else group
            for n, (held, _) in enumerate(pieces):
                if group in held:
                    at = held.index(group) * GROUP
                    return refs[2 * n + which][rows, at : at + GROUP]

        for n, b in enumerate(region):
            for q in range(lat):
                rows = slice(q * rank, (q + 1) * rank)
                sides = [
                    jnp.concatenate(
                        [part(b, w, rows), jnp.where(first_half, part(b + 1, w, rows), part(b - 1, w, rows))], axis=1
                    )
                    for w in range(2)
                ]
                total = jnp.dot(
                    jnp.concatenate(sides, axis=0),
                    k_refs[owners[n][0]][owners[n][1], :, q * GROUP : (q + 1) * GROUP],
                    preferred_element_type=jnp.float32,
                )
                out[rows, n * GROUP : (n + 1) * GROUP] = (total[:rank] + total[rank:]).astype(jnp.bfloat16)

    arrays = [a for _, pair in pieces for a in pair]
    count = len(region) * GROUP
    return pl.pallas_call(
        body,
        out_shape=shape((half, count), jnp.bfloat16),
        in_specs=[VM] * (len(kernels) + len(arrays)),
        out_specs=VM,
        compiler_params=grant(8),
        cost_estimate=cost(8 * half * GROUP * count, 4 * GROUP * lat * count),
        name="smooth",
    )(*kernels, *arrays)


def mix(smoothed, factors, nugget, values, product, region, mine):
    tasks = factors.shape[0]
    span, width = values.shape[1] // 2, len(region) * GROUP
    cuts = tiles(region)

    def body(s_ref, f_ref, g_ref, v_ref, *rest):
        o_hbm, o_buf, sems = rest[-3:]
        side = core_of() if mine else 1 - core_of()
        noise = jnp.broadcast_to(g_ref[...], (8, tasks)).T[:, :1]
        copies = []
        for i, (at, place, size) in enumerate(cuts):
            s, p = slice(place, place + size), columns(at, size, side, span)
            mixed = jnp.dot(f_ref[...], s_ref[:, s], preferred_element_type=jnp.float32)
            o_buf[:, s] = mixed + noise * v_ref[:, p].astype(jnp.float32)
            copies.append(pltpu.make_async_copy(o_buf.at[:, pl.ds(place, size)], o_hbm.at[:, p], sems.at[i]))
            copies[-1].start()
        for copy in copies:
            copy.wait()

    args = [smoothed, factors, nugget, values]
    specs = [VM, VM, VM, VM]
    alias = {}
    if product is not None:
        args.append(product)
        specs.append(HBM)
        alias = {4: 0}
    return pl.pallas_call(
        body,
        out_shape=shape(values.shape, jnp.float32),
        in_specs=specs,
        out_specs=HBM,
        scratch_shapes=[pltpu.VMEM((tasks, width), jnp.float32), pltpu.SemaphoreType.DMA((len(cuts),))],
        input_output_aliases=alias,
        compiler_params=grant(10),
        cost_estimate=cost(2 * tasks * factors.shape[1] * width, tasks * width * 4),
        name="mix",
    )(*args)


def runs(groups):
    found = []
    for g in groups:
        if found and found[-1][1] == g:
            found[-1][1] = g + 1
        else:
            found.append([g, g + 1])
    return found


def partners(size, bit):
    return [(i, i ^ bit) for i in range(size)]


def sum_fields(share, size):
    bit, other = 2, None
    while bit < size:
        if other is not None:
            share = (share.astype(jnp.float32) + other.astype(jnp.float32)).astype(jnp.bfloat16)
        other = lax.ppermute(share, "task", partners(size, bit))
        bit *= 2
    return share, other


def plan(groups):
    cuts = [1] + [groups * n // 32 for n in CUTS]
    regions = [list(range(a, b)) for a, b in zip(cuts[:-1], cuts[1:])]
    regions.append(list(range(cuts[-1], groups)) + [0])
    starts = [0] + [c + 1 for c in cuts[1:]] + [groups]
    chunks = [list(range(a, b)) for a, b in zip(starts[:-1], starts[1:])]
    return regions, chunks


def steps_of(values, factors, jitter, length_scales, nugget, neighbours):
    peers, blocks = lax.axis_size("task"), lax.axis_size("site")
    lat = length_scales.shape[0]
    rank = factors.shape[1] // lat
    groups = values.shape[1] // (2 * GROUP)
    regions, chunks = plan(groups)
    nugget = nugget.reshape(1, -1)

    def build(n):
        edge_offsets = outside if n == len(regions) - 1 else None
        return kernel_blocks(offsets, gaps, betas, edge_offsets, regions[n], groups)

    rest = [g for chunk in chunks[1:] for g in chunk]
    own, send = project(values, factors, chunks[0], False)
    received = lax.ppermute(send, "task", partners(peers, 1))
    offsets, gaps, betas = make_tables(jitter, neighbours.T, length_scales.reshape(1, -1))
    (share,) = add_cores(own, received, chunks[0], chunks[:1])
    sums = [sum_fields(share, peers)]
    own, send = project(values, factors, rest, True)
    received = lax.ppermute(send, "task", partners(peers, 1))
    shares = add_cores(own, received, rest, chunks[1:])
    for part in shares[:-1]:
        sums.append(sum_fields(part, peers))
    left_edge, right_edge = take_edges(share, shares[-1], offsets)
    ring = [[s * peers + t + c for s in range(blocks) for c in range(2)] for t in range(0, peers, 2)]
    up = [(r[i], r[(i + 1) % len(r)]) for r in ring for i in range(len(r))]
    down = [(j, i) for i, j in up]
    from_left = lax.ppermute(right_edge, ("site", "task"), up)
    from_right = lax.ppermute(left_edge, ("site", "task"), down)
    last, outside = close_ring(from_left, from_right, shares[-1])
    sums.append(sum_fields(last, peers))
    held_groups = chunks[:-1] + [chunks[-1] + [groups]]

    product = None
    for n, region in enumerate(regions):
        kernels = [build(n)]
        pieces = [(held_groups[n], sums[n])]
        if n > 0:
            pieces.append((held_groups[n - 1], sums[n - 1]))
        if n == len(regions) - 1:
            pieces.append((held_groups[0], sums[0]))
        smoothed = smooth(kernels, region, pieces, lat, rank, groups)
        other = lax.ppermute(smoothed, "task", partners(peers, 1))
        product = mix(smoothed, factors, nugget, values, product, region, True)
        product = mix(other, factors, nugget, values, product, region, False)
    return product


def solution(mesh):
    return jax.shard_map(
        steps_of,
        mesh=mesh,
        in_specs=(
            P("task", "site"),
            P("task", None),
            P(None, "site"),
            P(),
            P("task"),
            P("site", None),
        ),
        out_specs=P("task", "site"),
        check_vma=False,
    )
```

```python
import jax
import jax.numpy as jnp
from jax import lax
from jax.experimental import pallas as pl
from jax.experimental.pallas import tpu as pltpu
from jax.sharding import PartitionSpec as P


SIDE = 16
GROUP = 128
HALF = GROUP // 2
REACH = 3 * SIDE
KAPPA = 3.0**-0.25
FAR_AWAY = 1024.0
STEP = 512
EDGE_ROWS = 16
MIB = 1 << 20
CUTS = (8, 16, 23, 28)

VM = pl.BlockSpec(memory_space=pltpu.VMEM)
HBM = pl.BlockSpec(memory_space=pltpu.HBM)


def shape(dims, kind):
    return jax.ShapeDtypeStruct(dims, kind)


def in_hbm(x):
    return pltpu.with_memory_space_constraint(x, pltpu.HBM)


def grant(mib):
    return pltpu.CompilerParams(vmem_limit_bytes=mib * MIB)


def cost(flops, size):
    return pl.CostEstimate(flops=flops, bytes_accessed=size, transcendentals=0)


def tiles(groups, step=STEP):
    found, place = [], 0
    for begin, end in runs(groups):
        for at in range(begin * GROUP, end * GROUP, step):
            size = min(step, end * GROUP - at)
            found.append((at, place, size))
            place += size
    return found


def core_of():
    return lax.rem(lax.axis_index("task"), 2)


def columns(begin, size, side, span):
    return pl.ds(pl.multiple_of(side * span + begin, GROUP), size)


def project(values, factors, groups, resident):
    tasks, ranks = factors.shape
    span, width = values.shape[1] // 2, len(groups) * GROUP
    cuts = tiles(groups)

    def body(f_hbm, v_hbm, own_ref, send_ref, v_ref, f_ref, sems):
        core = core_of()
        first = pltpu.make_async_copy(f_hbm, f_ref, sems.at[2 * len(cuts)])
        first.start()
        work = [(send_ref, 1 - core, *cut) for cut in cuts] + [(own_ref, core, *cut) for cut in cuts]
        copies = [] if resident else [
            pltpu.make_async_copy(v_hbm.at[:, columns(at, size, side, span)], v_ref.at[i // len(cuts), :, pl.ds(place, size)], sems.at[i])
            for i, (_, side, at, place, size) in enumerate(work)
        ]
        for copy in copies:
            copy.start()
        first.wait()
        turned = f_ref[...].astype(jnp.float32).T.astype(jnp.bfloat16)
        for i, (out, side, at, place, size) in enumerate(work):
            s = slice(place, place + size)
            if resident:
                field = v_hbm[:, columns(at, size, side, span)]
            else:
                copies[i].wait()
                field = v_ref[i // len(cuts), :, s]
            out[:, s] = jnp.dot(turned, field, preferred_element_type=jnp.float32).astype(out.dtype)

    return pl.pallas_call(
        body,
        out_shape=(shape((ranks, width), jnp.float32), shape((ranks, width), jnp.bfloat16)),
        in_specs=[HBM, VM if resident else HBM],
        out_specs=(VM, VM),
        scratch_shapes=[
            pltpu.VMEM((1, 16, GROUP) if resident else (2, tasks, width), values.dtype),
            pltpu.VMEM(factors.shape, factors.dtype),
            pltpu.SemaphoreType.DMA((2 * len(cuts) + 1,)),
        ],
        compiler_params=grant(14),
        cost_estimate=cost(4 * tasks * ranks * width, tasks * width * 4),
        name="project",
    )(in_hbm(factors), values if resident else in_hbm(values))


def make_tables(jitter, neighbours, scales, nugget):
    span, owner, lat = jitter.shape[1] // 2, neighbours.shape[1], scales.shape[1]

    tasks = nugget.shape[1]

    def body(j_hbm, n_hbm, s_hbm, g_hbm, j_out, gap_out, beta_out, noise_out, n_ref, s_ref, g_ref, gap_ref, sems):
        core = core_of()
        copies = [
            pltpu.make_async_copy(j_hbm.at[:, columns(0, span, core, span)], j_out, sems.at[0]),
            pltpu.make_async_copy(n_hbm, n_ref, sems.at[1]),
            pltpu.make_async_copy(s_hbm, s_ref, sems.at[2]),
            pltpu.make_async_copy(g_hbm, g_ref, sems.at[3]),
        ]
        for copy in copies:
            copy.start()
        for copy in copies:
            copy.wait()
        noise_out[...] = jnp.broadcast_to(jnp.broadcast_to(g_ref[...], (8, tasks)).T[:, :1], (tasks, GROUP))
        lane = lax.broadcasted_iota(jnp.int32, (owner, GROUP), 1)
        for parity in range(2):
            cut = jnp.where(n_ref[parity + 1 : parity + 2, :] < 0, FAR_AWAY, 0.0)
            column = jnp.broadcast_to(cut, (8, owner)).T[:, :1]
            gap_ref[parity] = jnp.where((lane < HALF) == (parity == 0), jnp.broadcast_to(column, (owner, GROUP)), 0.0)
            mine = pl.multiple_of(core * (owner // 2), owner // 2)
            gap_out[parity] = gap_ref[parity, pl.ds(mine, owner // 2), :]
        scale = s_ref[...]
        which = lax.broadcasted_iota(jnp.int32, scale.shape, 1)
        beta = 1.0 / (KAPPA * scale * scale)
        for q in range(lat):
            value = jnp.sum(jnp.where(which == q, beta, 0.0), axis=1, keepdims=True)
            beta_out[8 * q : 8 * q + 8, :] = jnp.broadcast_to(value, (8, GROUP))

    return pl.pallas_call(
        body,
        out_shape=(
            shape((2, span), jitter.dtype),
            shape((2, owner // 2, GROUP), jnp.float32),
            shape((8 * lat, GROUP), jnp.float32),
            shape((tasks, GROUP), jnp.float32),
        ),
        in_specs=[HBM] * 4,
        out_specs=(VM, VM, VM, VM),
        scratch_shapes=[
            pltpu.VMEM(neighbours.shape, neighbours.dtype),
            pltpu.VMEM(scales.shape, scales.dtype),
            pltpu.VMEM(nugget.shape, nugget.dtype),
            pltpu.VMEM((2, owner, GROUP), jnp.float32),
            pltpu.SemaphoreType.DMA((4,)),
        ],
        compiler_params=grant(2),
        cost_estimate=cost(jitter.size, 4 * jitter.size),
        name="make_tables",
    )(in_hbm(jitter), in_hbm(neighbours), in_hbm(scales), in_hbm(nugget))


def add_cores(own, received, held, chunks):
    ranks = own.shape[0]

    def body(own_ref, got_ref, *outs):
        for groups, out in zip(chunks, outs):
            for begin, end in runs(groups):
                place = groups.index(begin) * GROUP
                s = slice(held.index(begin) * GROUP, held.index(end - 1) * GROUP + GROUP)
                total = own_ref[:, s] + got_ref[:, s].astype(jnp.float32)
                out[:, place : place + (end - begin) * GROUP] = total.astype(jnp.bfloat16)

    return pl.pallas_call(
        body,
        out_shape=[shape((ranks, len(groups) * GROUP), jnp.bfloat16) for groups in chunks],
        in_specs=[VM, VM],
        out_specs=[VM] * len(chunks),
        compiler_params=grant(8),
        cost_estimate=cost(own.size, own.size * 6),
        name="add_cores",
    )(own, received)


def take_edges(first, last, offsets):
    ranks = first.shape[0]

    def body(first_ref, last_ref, j_ref, *outs):
        for out, source, s in ((outs[0], first_ref, slice(0, GROUP)), (outs[1], last_ref, slice(-GROUP, None))):
            out[:ranks, :] = source[:, s]
            out[ranks:, :] = jnp.zeros((EDGE_ROWS, GROUP), jnp.bfloat16)
            out[ranks : ranks + 2, :] = j_ref[:, s]

    return pl.pallas_call(
        body,
        out_shape=[shape((ranks + EDGE_ROWS, GROUP), jnp.bfloat16)] * 2,
        in_specs=[VM] * 3,
        out_specs=[VM] * 2,
        compiler_params=grant(3),
        cost_estimate=cost(first.size, first.size),
        name="take_edges",
    )(first, last, offsets)


def close_ring(from_left, from_right, share):
    half, width = share.shape

    def body(left_ref, right_ref, share_ref, out, offsets):
        first_half = lax.broadcasted_iota(jnp.int32, (1, GROUP), 1) < HALF
        out[:, :width] = share_ref[...]
        out[:, width:] = jnp.where(first_half, right_ref[:half, :], left_ref[:half, :])
        offsets[...] = jnp.where(first_half, right_ref[half:, :], left_ref[half:, :])

    return pl.pallas_call(
        body,
        out_shape=(shape((half, width + GROUP), share.dtype), shape((EDGE_ROWS, GROUP), share.dtype)),
        in_specs=[VM, VM, VM],
        out_specs=(VM, VM),
        compiler_params=grant(2),
        cost_estimate=cost(share.size, 4 * share.size),
        name="close_ring",
    )(from_left, from_right, share)


def fill_blocks(region, groups, j_ref, gap_ref, beta_ref, edge_ref, k_ref):
    lat = beta_ref.shape[0] // 8
    rows = GROUP + REACH
    wide = 2 * GROUP
    sub = lax.broadcasted_iota(jnp.int32, (8, wide), 0)
    lane = lax.broadcasted_iota(jnp.int32, (8, wide), 1)
    row, col = ((lane >> 4).astype(jnp.float32), (lane & (SIDE - 1)).astype(jnp.float32))
    corner = lane >= GROUP
    past_row = jnp.where(corner, row - 11.0, row)
    zero = jnp.zeros_like(row)
    far_base = (
        jnp.where(sub == 1, past_row, jnp.where(sub == 4, row, jnp.where(sub >= 6, 1.0, zero))),
        jnp.where((sub == 1) | (sub == 4), col, jnp.where(sub >= 6, 1.0, zero)),
    )
    sub_1, lane_1 = sub[:, :GROUP], lane[:, :GROUP]
    meets = jnp.where((sub_1 < 3) == (lane_1 < HALF), 1.0, 0.0)
    own_base = tuple(jnp.where(sub_1 < 6, meets, -base[:, :GROUP]) for base in (row, col))
    none = jnp.zeros((8, GROUP), jnp.float32)
    first_half = lax.broadcasted_iota(jnp.int32, (1, GROUP), 1) < HALF
    scale = [beta_ref[8 * q : 8 * q + 1, :] for q in range(lat)]

    def offsets_of(b):
        if isinstance(b, int):
            return j_ref[:, b * GROUP : (b + 1) * GROUP].astype(jnp.float32)
        return j_ref[:, pl.ds(pl.multiple_of(b * GROUP, GROUP), GROUP)].astype(jnp.float32)

    def eight(x):
        return jnp.broadcast_to(x, (8, GROUP))

    def block(b, parity, slot):
        here = offsets_of(b)
        before = edge_ref[:2, :].astype(jnp.float32) if isinstance(b, int) and b == 0 else offsets_of(b - 1)
        after = edge_ref[:2, :].astype(jnp.float32) if isinstance(b, int) and b == groups - 1 else offsets_of(b + 1)
        gap = eight(gap_ref[parity, pl.ds(b // 2, 1), :])
        far, own = [], []
        for axis in range(2):
            mine = eight(here[axis : axis + 1])
            past = pltpu.roll(eight(before[axis : axis + 1]), REACH, 1)
            coming = eight(after[axis : axis + 1])
            base = far_base[axis]
            left = jnp.where((sub_1 == 0) | (sub_1 == 3), mine, base[:, :GROUP])
            right = jnp.where(sub_1 == 0, past, jnp.where(sub_1 == 3, coming, base[:, GROUP:]))
            if axis == 0 and parity == 0:
                right = jnp.where(sub_1 == 2, gap, right)
            if axis == 0 and parity == 1:
                right = jnp.where(sub_1 == 5, pltpu.roll(gap, HALF, 1), right)
            far.append(jnp.concatenate([left, right], axis=1))
            own.append(jnp.where(sub_1 == 6, -mine, own_base[axis]))
        left = jnp.concatenate(far, axis=0).T[:rows].astype(jnp.bfloat16)
        right = jnp.concatenate(
            [jnp.concatenate([own[0], none], axis=1), jnp.concatenate([none, own[1]], axis=1)], axis=0
        ).astype(jnp.bfloat16)
        away = jnp.dot(left, right, preferred_element_type=jnp.float32)
        across, sideways = away[:, :GROUP], away[:, GROUP:]
        distance = across * across + sideways * sideways
        for q in range(lat):
            u = jnp.maximum(1.0 / KAPPA - scale[q] * distance, 0.0)
            weight = (u * u * u * (4.0 * KAPPA**3 - u)).astype(jnp.bfloat16)
            s = slice(q * GROUP, (q + 1) * GROUP)
            blank = jnp.zeros((REACH, GROUP), jnp.bfloat16)
            k_ref[slot, :GROUP, s] = weight[:GROUP]
            k_ref[slot, GROUP : GROUP + REACH, s] = jnp.where(first_half, blank, weight[GROUP:])
            k_ref[slot, wide - REACH :, s] = jnp.where(first_half, weight[GROUP:], blank)
        k_ref[slot, GROUP + REACH : wide - REACH, :] = jnp.zeros((GROUP - 2 * REACH, lat * GROUP), jnp.bfloat16)

    count = 4
    for begin, end in runs(region):
        slot = region.index(begin)
        low, high = begin + (begin == 0), end - (end == groups)
        low = min(low + low % 2, end)
        for b in range(begin, low):
            block(b, b % 2, slot + b - begin)
        whole = (high - low) // count

        def several(i, carry, low=low, shift=slot - begin):
            for m in range(count):
                b = low + i * count + m
                block(b, m % 2, b + shift)
            return carry

        if whole > 1:
            lax.fori_loop(0, whole, several, 0)
        else:
            whole = 0
        for b in range(low + whole * count, end):
            block(b, b % 2, slot + b - begin)


def kernel_blocks(tables, edges, region, groups):
    args = list(tables) + ([edges] if edges is not None else [])

    def body(*refs):
        fill_blocks(region, groups, *refs[:3], refs[3], refs[-1])

    return pl.pallas_call(
        body,
        out_shape=block_shape(tables, region),
        in_specs=[VM] * len(args),
        out_specs=VM,
        compiler_params=grant(6),
        cost_estimate=block_cost(tables, region),
        name="kernel_blocks",
    )(*args)


def block_shape(tables, region):
    return shape((len(region), 2 * GROUP, tables[2].shape[0] // 8 * GROUP), jnp.bfloat16)


def block_cost(tables, region):
    size = block_shape(tables, region).size
    return cost(30 * size, 2 * size)


def smooth(kernels, region, pieces, lat, rank, groups):
    half = lat * rank
    owners = [(k, m) for k, kernel in enumerate(kernels) for m in range(kernel.shape[0])]

    def body(*refs):
        k_refs, refs = refs[: len(kernels)], refs[len(kernels) :]
        out = refs[-1]
        first_half = lax.broadcasted_iota(jnp.int32, (1, GROUP), 1) < HALF

        def part(group, which, rows):
            group = groups if group < 0 else group
            for n, (held, _) in enumerate(pieces):
                if group in held:
                    at = held.index(group) * GROUP
                    return refs[2 * n + which][rows, at : at + GROUP]

        for n, b in enumerate(region):
            for q in range(lat):
                rows = slice(q * rank, (q + 1) * rank)
                sides = [
                    jnp.concatenate(
                        [part(b, w, rows), jnp.where(first_half, part(b + 1, w, rows), part(b - 1, w, rows))], axis=1
                    )
                    for w in range(2)
                ]
                total = jnp.dot(
                    jnp.concatenate(sides, axis=0),
                    k_refs[owners[n][0]][owners[n][1], :, q * GROUP : (q + 1) * GROUP],
                    preferred_element_type=jnp.float32,
                )
                out[rows, n * GROUP : (n + 1) * GROUP] = (total[:rank] + total[rank:]).astype(jnp.bfloat16)

    arrays = [a for _, pair in pieces for a in pair]
    count = len(region) * GROUP
    return pl.pallas_call(
        body,
        out_shape=shape((half, count), jnp.bfloat16),
        in_specs=[VM] * (len(kernels) + len(arrays)),
        out_specs=VM,
        compiler_params=grant(8),
        cost_estimate=cost(8 * half * GROUP * count, 4 * GROUP * lat * count),
        name="smooth",
    )(*kernels, *arrays)


def mix(smoothed, factors, noise, values, product, region, mine, more=None):
    tasks = factors.shape[0]
    span, width = values.shape[1] // 2, len(region) * GROUP
    cuts = tiles(region, GROUP)

    def body(s_ref, f_ref, g_ref, v_ref, *rest):
        o_buf, sems = rest[-2:]
        o_hbm = rest[-4] if more else rest[-3]
        side = core_of() if mine else 1 - core_of()
        copies = []
        for i, (at, place, size) in enumerate(cuts):
            s, p = slice(place, place + size), columns(at, size, side, span)
            mixed = jnp.dot(f_ref[...], s_ref[:, s], preferred_element_type=jnp.float32)
            o_buf[:, s] = mixed + g_ref[...] * v_ref[:, p].astype(jnp.float32)
            copies.append(pltpu.make_async_copy(o_buf.at[:, pl.ds(place, size)], o_hbm.at[:, p], sems.at[i]))
            copies[-1].start()
        if more:
            fill_blocks(more[2], more[3], *rest[:3], rest[3], rest[-3])
        for copy in copies:
            copy.wait()

    args = [smoothed, factors, noise, values]
    out, out_specs = [shape(values.shape, jnp.float32)], [HBM]
    price = cost(2 * tasks * factors.shape[1] * width, tasks * width * 4)
    if more:
        args += list(more[0]) + ([more[1]] if more[1] is not None else [])
        out.append(block_shape(more[0], more[2]))
        out_specs.append(VM)
        built = block_cost(more[0], more[2])
        price = cost(price.flops + built.flops, price.bytes_accessed + built.bytes_accessed)
    specs = [VM] * len(args)
    alias = {}
    if product is not None:
        alias = {len(args): 0}
        args.append(product)
        specs.append(HBM)
    return pl.pallas_call(
        body,
        out_shape=out,
        in_specs=specs,
        out_specs=out_specs,
        scratch_shapes=[pltpu.VMEM((tasks, width), jnp.float32), pltpu.SemaphoreType.DMA((len(cuts),))],
        input_output_aliases=alias,
        compiler_params=grant(12),
        cost_estimate=price,
        name="mix",
    )(*args)


def runs(groups):
    found = []
    for g in groups:
        if found and found[-1][1] == g:
            found[-1][1] = g + 1
        else:
            found.append([g, g + 1])
    return found


def partners(size, bit):
    return [(i, i ^ bit) for i in range(size)]


def sum_fields(share, size):
    bit, other = 2, None
    while bit < size:
        if other is not None:
            share = (share.astype(jnp.float32) + other.astype(jnp.float32)).astype(jnp.bfloat16)
        other = lax.ppermute(share, "task", partners(size, bit))
        bit *= 2
    return share, other


def plan(groups):
    cuts = [1] + [groups * n // 32 for n in CUTS]
    regions = [list(range(a, b)) for a, b in zip(cuts[:-1], cuts[1:])]
    regions.append(list(range(cuts[-1], groups)) + [0])
    starts = [0] + [c + 1 for c in cuts[1:]] + [groups]
    chunks = [list(range(a, b)) for a, b in zip(starts[:-1], starts[1:])]
    return regions, chunks


def steps_of(values, factors, jitter, length_scales, nugget, neighbours):
    peers, blocks = lax.axis_size("task"), lax.axis_size("site")
    lat = length_scales.shape[0]
    rank = factors.shape[1] // lat
    groups = values.shape[1] // (2 * GROUP)
    regions, chunks = plan(groups)
    rest = [g for chunk in chunks[1:] for g in chunk]
    own, send = project(values, factors, chunks[0], False)
    received = lax.ppermute(send, "task", partners(peers, 1))
    *tables, noise = make_tables(jitter, neighbours.T, length_scales.reshape(1, -1), nugget.reshape(1, -1))
    (share,) = add_cores(own, received, chunks[0], chunks[:1])
    sums = [sum_fields(share, peers)]
    own, send = project(values, factors, rest, True)
    received = lax.ppermute(send, "task", partners(peers, 1))
    shares = add_cores(own, received, rest, chunks[1:])
    for part in shares[:-1]:
        sums.append(sum_fields(part, peers))
    left_edge, right_edge = take_edges(share, shares[-1], tables[0])
    ring = [[s * peers + t + c for s in range(blocks) for c in range(2)] for t in range(0, peers, 2)]
    up = [(r[i], r[(i + 1) % len(r)]) for r in ring for i in range(len(r))]
    down = [(j, i) for i, j in up]
    from_left = lax.ppermute(right_edge, ("site", "task"), up)
    from_right = lax.ppermute(left_edge, ("site", "task"), down)
    last, outside = close_ring(from_left, from_right, shares[-1])
    sums.append(sum_fields(last, peers))
    held_groups = chunks[:-1] + [chunks[-1] + [groups]]

    final = len(regions) - 1
    parts = dict(zip(("mix0", "mix0b", "mix1", "mix1b"), regions[1:]))
    kernels = [[] for _ in regions]
    kernels[0].append(kernel_blocks(tables, None, regions[0], groups))

    product = None
    for n, region in enumerate(regions):
        pieces = [(held_groups[n], sums[n])]
        if n > 0:
            pieces.append((held_groups[n - 1], sums[n - 1]))
        if n == final:
            pieces.append((held_groups[0], sums[0]))
        smoothed = smooth(kernels[n], region, pieces, lat, rank, groups)
        other = lax.ppermute(smoothed, "task", partners(peers, 1))
        for name, rows, mine in ((f"mix{n}", smoothed, True), (f"mix{n}b", other, False)):
            part = parts.get(name)
            more = part and (tables, outside if part is regions[final] else None, part, groups)
            product, *built = mix(rows, factors, noise, values, product, region, mine, more)
            if built:
                kernels[regions.index(part)].append(built[0])
    return product


def solution(mesh):
    return jax.shard_map(
        steps_of,
        mesh=mesh,
        in_specs=(
            P("task", "site"),
            P("task", None),
            P(None, "site"),
            P(),
            P("task"),
            P("site", None),
        ),
        out_specs=P("task", "site"),
        check_vma=False,
    )
```

```python
import jax
import jax.numpy as jnp
from jax import lax
from jax.experimental import pallas as pl
from jax.experimental.pallas import tpu as pltpu
from jax.sharding import PartitionSpec as P


SIDE = 16
GROUP = 128
HALF = GROUP // 2
REACH = 3 * SIDE
KAPPA = 3.0**-0.25
FAR_AWAY = 1024.0
STEP = 512
EDGE_ROWS = 16
MIB = 1 << 20
CUTS = (9, 20, 27)

VM = pl.BlockSpec(memory_space=pltpu.VMEM)
HBM = pl.BlockSpec(memory_space=pltpu.HBM)


def shape(dims, kind):
    return jax.ShapeDtypeStruct(dims, kind)


def in_hbm(x):
    return pltpu.with_memory_space_constraint(x, pltpu.HBM)


def grant(mib):
    return pltpu.CompilerParams(vmem_limit_bytes=mib * MIB)


def cost(flops, size):
    return pl.CostEstimate(flops=flops, bytes_accessed=size, transcendentals=0)


def tiles(groups, step=STEP):
    found, place = [], 0
    for begin, end in runs(groups):
        for at in range(begin * GROUP, end * GROUP, step):
            size = min(step, end * GROUP - at)
            found.append((at, place, size))
            place += size
    return found


def core_of():
    return lax.rem(lax.axis_index("task"), 2)


def columns(begin, size, side, span):
    return pl.ds(pl.multiple_of(side * span + begin, GROUP), size)


def project(values, factors, groups, resident):
    tasks, ranks = factors.shape
    span, width = values.shape[1] // 2, len(groups) * GROUP
    cuts = tiles(groups, 2 * STEP if resident else width)

    def body(f_hbm, v_hbm, own_ref, send_ref, v_ref, f_ref, sems):
        core = core_of()
        first = pltpu.make_async_copy(f_hbm, f_ref, sems.at[2 * len(cuts)])
        first.start()
        work = [(send_ref, 1 - core, *cut) for cut in cuts] + [(own_ref, core, *cut) for cut in cuts]
        copies = [] if resident else [
            pltpu.make_async_copy(v_hbm.at[:, columns(at, size, side, span)], v_ref.at[i // len(cuts), :, pl.ds(place, size)], sems.at[i])
            for i, (_, side, at, place, size) in enumerate(work)
        ]
        for copy in copies:
            copy.start()
        first.wait()
        turned = f_ref[...].astype(jnp.float32).T.astype(jnp.bfloat16)
        for i, (out, side, at, place, size) in enumerate(work):
            s = slice(place, place + size)
            if resident:
                field = v_hbm[:, columns(at, size, side, span)]
            else:
                copies[i].wait()
                field = v_ref[i // len(cuts), :, s]
            out[:, s] = jnp.dot(turned, field, preferred_element_type=jnp.float32).astype(out.dtype)

    return pl.pallas_call(
        body,
        out_shape=(shape((ranks, width), jnp.float32), shape((ranks, width), jnp.bfloat16)),
        in_specs=[HBM, VM if resident else HBM],
        out_specs=(VM, VM),
        scratch_shapes=[
            pltpu.VMEM((1, 16, GROUP) if resident else (2, tasks, width), values.dtype),
            pltpu.VMEM(factors.shape, factors.dtype),
            pltpu.SemaphoreType.DMA((2 * len(cuts) + 1,)),
        ],
        compiler_params=grant(14),
        cost_estimate=cost(4 * tasks * ranks * width, tasks * width * 4),
        name="project",
    )(in_hbm(factors), values if resident else in_hbm(values))


def make_tables(jitter, neighbours, scales, nugget):
    span, owner, lat = jitter.shape[1] // 2, neighbours.shape[1], scales.shape[1]

    tasks = nugget.shape[1]

    def body(j_hbm, n_hbm, s_hbm, g_hbm, j_out, gap_out, beta_out, noise_out, n_ref, s_ref, g_ref, gap_ref, sems):
        core = core_of()
        copies = [
            pltpu.make_async_copy(j_hbm.at[:, columns(0, span, core, span)], j_out, sems.at[0]),
            pltpu.make_async_copy(n_hbm, n_ref, sems.at[1]),
            pltpu.make_async_copy(s_hbm, s_ref, sems.at[2]),
            pltpu.make_async_copy(g_hbm, g_ref, sems.at[3]),
        ]
        for copy in copies:
            copy.start()
        for copy in copies:
            copy.wait()
        noise_out[...] = jnp.broadcast_to(jnp.broadcast_to(g_ref[...], (8, tasks)).T[:, :1], (tasks, GROUP))
        lane = lax.broadcasted_iota(jnp.int32, (owner, GROUP), 1)
        for parity in range(2):
            cut = jnp.where(n_ref[parity + 1 : parity + 2, :] < 0, FAR_AWAY, 0.0)
            column = jnp.broadcast_to(cut, (8, owner)).T[:, :1]
            gap_ref[parity] = jnp.where((lane < HALF) == (parity == 0), jnp.broadcast_to(column, (owner, GROUP)), 0.0)
            mine = pl.multiple_of(core * (owner // 2), owner // 2)
            gap_out[parity] = gap_ref[parity, pl.ds(mine, owner // 2), :]
        scale = s_ref[...]
        which = lax.broadcasted_iota(jnp.int32, scale.shape, 1)
        beta = 1.0 / (KAPPA * scale * scale)
        for q in range(lat):
            value = jnp.sum(jnp.where(which == q, beta, 0.0), axis=1, keepdims=True)
            beta_out[8 * q : 8 * q + 8, :] = jnp.broadcast_to(value, (8, GROUP))

    return pl.pallas_call(
        body,
        out_shape=(
            shape((2, span), jitter.dtype),
            shape((2, owner // 2, GROUP), jnp.float32),
            shape((8 * lat, GROUP), jnp.float32),
            shape((tasks, GROUP), jnp.float32),
        ),
        in_specs=[HBM] * 4,
        out_specs=(VM, VM, VM, VM),
        scratch_shapes=[
            pltpu.VMEM(neighbours.shape, neighbours.dtype),
            pltpu.VMEM(scales.shape, scales.dtype),
            pltpu.VMEM(nugget.shape, nugget.dtype),
            pltpu.VMEM((2, owner, GROUP), jnp.float32),
            pltpu.SemaphoreType.DMA((4,)),
        ],
        compiler_params=grant(2),
        cost_estimate=cost(jitter.size, 4 * jitter.size),
        name="make_tables",
    )(in_hbm(jitter), in_hbm(neighbours), in_hbm(scales), in_hbm(nugget))


def add_cores(own, received, held, chunks):
    ranks = own.shape[0]

    def body(own_ref, got_ref, *outs):
        for groups, out in zip(chunks, outs):
            for begin, end in runs(groups):
                place = groups.index(begin) * GROUP
                s = slice(held.index(begin) * GROUP, held.index(end - 1) * GROUP + GROUP)
                total = own_ref[:, s] + got_ref[:, s].astype(jnp.float32)
                out[:, place : place + (end - begin) * GROUP] = total.astype(jnp.bfloat16)

    return pl.pallas_call(
        body,
        out_shape=[shape((ranks, len(groups) * GROUP), jnp.bfloat16) for groups in chunks],
        in_specs=[VM, VM],
        out_specs=[VM] * len(chunks),
        compiler_params=grant(8),
        cost_estimate=cost(own.size, own.size * 6),
        name="add_cores",
    )(own, received)


def take_edges(first, last, offsets):
    ranks = first.shape[0]

    def body(first_ref, last_ref, j_ref, *outs):
        for out, source, s in ((outs[0], first_ref, slice(0, GROUP)), (outs[1], last_ref, slice(-GROUP, None))):
            out[:ranks, :] = source[:, s]
            out[ranks:, :] = jnp.zeros((EDGE_ROWS, GROUP), jnp.bfloat16)
            out[ranks : ranks + 2, :] = j_ref[:, s]

    return pl.pallas_call(
        body,
        out_shape=[shape((ranks + EDGE_ROWS, GROUP), jnp.bfloat16)] * 2,
        in_specs=[VM] * 3,
        out_specs=[VM] * 2,
        compiler_params=grant(3),
        cost_estimate=cost(first.size, first.size),
        name="take_edges",
    )(first, last, offsets)


def close_ring(from_left, from_right, share):
    half, width = share.shape

    def body(left_ref, right_ref, share_ref, out, offsets):
        first_half = lax.broadcasted_iota(jnp.int32, (1, GROUP), 1) < HALF
        out[:, :width] = share_ref[...]
        out[:, width:] = jnp.where(first_half, right_ref[:half, :], left_ref[:half, :])
        offsets[...] = jnp.where(first_half, right_ref[half:, :], left_ref[half:, :])

    return pl.pallas_call(
        body,
        out_shape=(shape((half, width + GROUP), share.dtype), shape((EDGE_ROWS, GROUP), share.dtype)),
        in_specs=[VM, VM, VM],
        out_specs=(VM, VM),
        compiler_params=grant(2),
        cost_estimate=cost(share.size, 4 * share.size),
        name="close_ring",
    )(from_left, from_right, share)


def fill_blocks(region, groups, j_ref, gap_ref, beta_ref, edge_ref, k_ref):
    lat = beta_ref.shape[0] // 8
    rows = GROUP + REACH
    wide = 2 * GROUP
    sub = lax.broadcasted_iota(jnp.int32, (8, wide), 0)
    lane = lax.broadcasted_iota(jnp.int32, (8, wide), 1)
    row, col = ((lane >> 4).astype(jnp.float32), (lane & (SIDE - 1)).astype(jnp.float32))
    corner = lane >= GROUP
    past_row = jnp.where(corner, row - 11.0, row)
    zero = jnp.zeros_like(row)
    far_base = (
        jnp.where(sub == 1, past_row, jnp.where(sub == 4, row, jnp.where(sub >= 6, 1.0, zero))),
        jnp.where((sub == 1) | (sub == 4), col, jnp.where(sub >= 6, 1.0, zero)),
    )
    sub_1, lane_1 = sub[:, :GROUP], lane[:, :GROUP]
    meets = jnp.where((sub_1 < 3) == (lane_1 < HALF), 1.0, 0.0)
    own_base = tuple(jnp.where(sub_1 < 6, meets, -base[:, :GROUP]) for base in (row, col))
    none = jnp.zeros((8, GROUP), jnp.float32)
    first_half = lax.broadcasted_iota(jnp.int32, (1, GROUP), 1) < HALF
    scale = [beta_ref[8 * q : 8 * q + 1, :] for q in range(lat)]

    def offsets_of(b):
        if isinstance(b, int):
            return j_ref[:, b * GROUP : (b + 1) * GROUP].astype(jnp.float32)
        return j_ref[:, pl.ds(pl.multiple_of(b * GROUP, GROUP), GROUP)].astype(jnp.float32)

    def eight(x):
        return jnp.broadcast_to(x, (8, GROUP))

    def block(b, parity, slot):
        here = offsets_of(b)
        before = edge_ref[:2, :].astype(jnp.float32) if isinstance(b, int) and b == 0 else offsets_of(b - 1)
        after = edge_ref[:2, :].astype(jnp.float32) if isinstance(b, int) and b == groups - 1 else offsets_of(b + 1)
        gap = eight(gap_ref[parity, pl.ds(b // 2, 1), :])
        far, own = [], []
        for axis in range(2):
            mine = eight(here[axis : axis + 1])
            past = pltpu.roll(eight(before[axis : axis + 1]), REACH, 1)
            coming = eight(after[axis : axis + 1])
            base = far_base[axis]
            left = jnp.where((sub_1 == 0) | (sub_1 == 3), mine, base[:, :GROUP])
            right = jnp.where(sub_1 == 0, past, jnp.where(sub_1 == 3, coming, base[:, GROUP:]))
            if axis == 0 and parity == 0:
                right = jnp.where(sub_1 == 2, gap, right)
            if axis == 0 and parity == 1:
                right = jnp.where(sub_1 == 5, pltpu.roll(gap, HALF, 1), right)
            far.append(jnp.concatenate([left, right], axis=1))
            own.append(jnp.where(sub_1 == 6, -mine, own_base[axis]))
        left = jnp.concatenate(far, axis=0).T[:rows].astype(jnp.bfloat16)
        right = jnp.concatenate(
            [jnp.concatenate([own[0], none], axis=1), jnp.concatenate([none, own[1]], axis=1)], axis=0
        ).astype(jnp.bfloat16)
        away = jnp.dot(left, right, preferred_element_type=jnp.float32)
        across, sideways = away[:, :GROUP], away[:, GROUP:]
        distance = across * across + sideways * sideways
        for q in range(lat):
            u = jnp.maximum(1.0 / KAPPA - scale[q] * distance, 0.0)
            weight = (u * u * u * (4.0 * KAPPA**3 - u)).astype(jnp.bfloat16)
            s = slice(q * GROUP, (q + 1) * GROUP)
            blank = jnp.zeros((REACH, GROUP), jnp.bfloat16)
            k_ref[slot, :GROUP, s] = weight[:GROUP]
            k_ref[slot, GROUP : GROUP + REACH, s] = jnp.where(first_half, blank, weight[GROUP:])
            k_ref[slot, wide - REACH :, s] = jnp.where(first_half, weight[GROUP:], blank)
        k_ref[slot, GROUP + REACH : wide - REACH, :] = jnp.zeros((GROUP - 2 * REACH, lat * GROUP), jnp.bfloat16)

    count = 4
    for begin, end in runs(region):
        slot = region.index(begin)
        low, high = begin + (begin == 0), end - (end == groups)
        low = min(low + low % 2, end)
        for b in range(begin, low):
            block(b, b % 2, slot + b - begin)
        whole = (high - low) // count

        def several(i, carry, low=low, shift=slot - begin):
            for m in range(count):
                b = low + i * count + m
                block(b, m % 2, b + shift)
            return carry

        if whole > 1:
            lax.fori_loop(0, whole, several, 0)
        else:
            whole = 0
        for b in range(low + whole * count, end):
            block(b, b % 2, slot + b - begin)


def kernel_blocks(tables, edges, region, groups):
    args = list(tables) + ([edges] if edges is not None else [])

    def body(*refs):
        fill_blocks(region, groups, *refs[:3], refs[3], refs[-1])

    return pl.pallas_call(
        body,
        out_shape=block_shape(tables, region),
        in_specs=[VM] * len(args),
        out_specs=VM,
        compiler_params=grant(6),
        cost_estimate=block_cost(tables, region),
        name="kernel_blocks",
    )(*args)


def block_shape(tables, region):
    return shape((len(region), 2 * GROUP, tables[2].shape[0] // 8 * GROUP), jnp.bfloat16)


def block_cost(tables, region):
    size = block_shape(tables, region).size
    return cost(30 * size, 2 * size)


def smooth(kernels, region, pieces, lat, rank, groups):
    half = lat * rank
    owners = [(k, m) for k, kernel in enumerate(kernels) for m in range(kernel.shape[0])]

    def body(*refs):
        k_refs, refs = refs[: len(kernels)], refs[len(kernels) :]
        out = refs[-1]
        first_half = lax.broadcasted_iota(jnp.int32, (1, GROUP), 1) < HALF

        def part(group, which, rows):
            group = groups if group < 0 else group
            for n, (held, _) in enumerate(pieces):
                if group in held:
                    at = held.index(group) * GROUP
                    return refs[2 * n + which][rows, at : at + GROUP]

        for n, b in enumerate(region):
            for q in range(lat):
                rows = slice(q * rank, (q + 1) * rank)
                sides = [
                    jnp.concatenate(
                        [part(b, w, rows), jnp.where(first_half, part(b + 1, w, rows), part(b - 1, w, rows))], axis=1
                    )
                    for w in range(2)
                ]
                total = jnp.dot(
                    jnp.concatenate(sides, axis=0),
                    k_refs[owners[n][0]][owners[n][1], :, q * GROUP : (q + 1) * GROUP],
                    preferred_element_type=jnp.float32,
                )
                out[rows, n * GROUP : (n + 1) * GROUP] = (total[:rank] + total[rank:]).astype(jnp.bfloat16)

    arrays = [a for _, pair in pieces for a in pair]
    count = len(region) * GROUP
    return pl.pallas_call(
        body,
        out_shape=shape((half, count), jnp.bfloat16),
        in_specs=[VM] * (len(kernels) + len(arrays)),
        out_specs=VM,
        compiler_params=grant(8),
        cost_estimate=cost(8 * half * GROUP * count, 4 * GROUP * lat * count),
        name="smooth",
    )(*kernels, *arrays)


def mix(smoothed, factors, noise, values, product, region, mine, more=None):
    tasks = factors.shape[0]
    span, width = values.shape[1] // 2, len(region) * GROUP
    cuts = tiles(region, GROUP)

    def body(s_ref, f_ref, g_ref, v_ref, *rest):
        o_buf, sems = rest[-2:]
        o_hbm = rest[-4] if more else rest[-3]
        side = core_of() if mine else 1 - core_of()
        copies = []
        for i, (at, place, size) in enumerate(cuts):
            s, p = slice(place, place + size), columns(at, size, side, span)
            mixed = jnp.dot(f_ref[...], s_ref[:, s], preferred_element_type=jnp.float32)
            o_buf[:, s] = mixed + g_ref[...] * v_ref[:, p].astype(jnp.float32)
            copies.append(pltpu.make_async_copy(o_buf.at[:, pl.ds(place, size)], o_hbm.at[:, p], sems.at[i]))
            copies[-1].start()
        if more:
            fill_blocks(more[2], more[3], *rest[:3], rest[3], rest[-3])
        for copy in copies:
            copy.wait()

    args = [smoothed, factors, noise, values]
    out, out_specs = [shape(values.shape, jnp.float32)], [HBM]
    price = cost(2 * tasks * factors.shape[1] * width, tasks * width * 4)
    if more:
        args += list(more[0]) + ([more[1]] if more[1] is not None else [])
        out.append(block_shape(more[0], more[2]))
        out_specs.append(VM)
        built = block_cost(more[0], more[2])
        price = cost(price.flops + built.flops, price.bytes_accessed + built.bytes_accessed)
    specs = [VM] * len(args)
    alias = {}
    if product is not None:
        alias = {len(args): 0}
        args.append(product)
        specs.append(HBM)
    return pl.pallas_call(
        body,
        out_shape=out,
        in_specs=specs,
        out_specs=out_specs,
        scratch_shapes=[pltpu.VMEM((tasks, width), jnp.float32), pltpu.SemaphoreType.DMA((len(cuts),))],
        input_output_aliases=alias,
        compiler_params=grant(12),
        cost_estimate=price,
        name="mix",
    )(*args)


def runs(groups):
    found = []
    for g in groups:
        if found and found[-1][1] == g:
            found[-1][1] = g + 1
        else:
            found.append([g, g + 1])
    return found


def partners(size, bit):
    return [(i, i ^ bit) for i in range(size)]


def sum_fields(share, size):
    bit, other = 2, None
    while bit < size:
        if other is not None:
            share = (share.astype(jnp.float32) + other.astype(jnp.float32)).astype(jnp.bfloat16)
        other = lax.ppermute(share, "task", partners(size, bit))
        bit *= 2
    return share, other


def plan(groups):
    cuts = [1] + [groups * n // 32 for n in CUTS]
    regions = [list(range(a, b)) for a, b in zip(cuts[:-1], cuts[1:])]
    regions.append(list(range(cuts[-1], groups)) + [0])
    starts = [0] + [c + 1 for c in cuts[1:]] + [groups]
    chunks = [list(range(a, b)) for a, b in zip(starts[:-1], starts[1:])]
    return regions, chunks


def steps_of(values, factors, jitter, length_scales, nugget, neighbours):
    peers, blocks = lax.axis_size("task"), lax.axis_size("site")
    lat = length_scales.shape[0]
    rank = factors.shape[1] // lat
    groups = values.shape[1] // (2 * GROUP)
    regions, chunks = plan(groups)
    rest = [g for chunk in chunks[1:] for g in chunk]
    own, send = project(values, factors, chunks[0], False)
    received = lax.ppermute(send, "task", partners(peers, 1))
    *tables, noise = make_tables(jitter, neighbours.T, length_scales.reshape(1, -1), nugget.reshape(1, -1))
    (share,) = add_cores(own, received, chunks[0], chunks[:1])
    sums = [sum_fields(share, peers)]
    own, send = project(values, factors, rest, True)
    received = lax.ppermute(send, "task", partners(peers, 1))
    shares = add_cores(own, received, rest, chunks[1:])
    for part in shares[:-1]:
        sums.append(sum_fields(part, peers))
    left_edge, right_edge = take_edges(share, shares[-1], tables[0])
    ring = [[s * peers + t + c for s in range(blocks) for c in range(2)] for t in range(0, peers, 2)]
    up = [(r[i], r[(i + 1) % len(r)]) for r in ring for i in range(len(r))]
    down = [(j, i) for i, j in up]
    from_left = lax.ppermute(right_edge, ("site", "task"), up)
    from_right = lax.ppermute(left_edge, ("site", "task"), down)
    last, outside = close_ring(from_left, from_right, shares[-1])
    sums.append(sum_fields(last, peers))
    held_groups = chunks[:-1] + [chunks[-1] + [groups]]

    final = len(regions) - 1
    middle = len(regions[1]) // 2
    parts = {"mix0": regions[1][:middle], "mix0b": regions[1][middle:], "mix1": regions[2], "mix1b": regions[3]}
    kernels = [[] for _ in regions]
    kernels[0].append(kernel_blocks(tables, None, regions[0], groups))

    product = None
    for n, region in enumerate(regions):
        pieces = [(held_groups[n], sums[n])]
        if n > 0:
            pieces.append((held_groups[n - 1], sums[n - 1]))
        if n == final:
            pieces.append((held_groups[0], sums[0]))
        smoothed = smooth(kernels[n], region, pieces, lat, rank, groups)
        other = lax.ppermute(smoothed, "task", partners(peers, 1))
        for name, rows, mine in ((f"mix{n}", smoothed, True), (f"mix{n}b", other, False)):
            part = parts.get(name)
            more = part and (tables, outside if part is regions[final] else None, part, groups)
            product, *built = mix(rows, factors, noise, values, product, region, mine, more)
            if built:
                kernels[1 if part[0] in regions[1] else regions.index(part)].append(built[0])
    return product


def solution(mesh):
    return jax.shard_map(
        steps_of,
        mesh=mesh,
        in_specs=(
            P("task", "site"),
            P("task", None),
            P(None, "site"),
            P(),
            P("task"),
            P("site", None),
        ),
        out_specs=P("task", "site"),
        check_vma=False,
    )
```

```python
import jax
import jax.numpy as jnp
from jax import lax
from jax.experimental import pallas as pl
from jax.experimental.pallas import tpu as pltpu
from jax.sharding import PartitionSpec as P


SIDE = 16
GROUP = 128
HALF = GROUP // 2
REACH = 3 * SIDE
KAPPA = 3.0**-0.25
FAR_AWAY = 1024.0
STEP = 512
EDGE_ROWS = 16
MIB = 1 << 20
CUTS = (7, 20, 27)

VM = pl.BlockSpec(memory_space=pltpu.VMEM)
HBM = pl.BlockSpec(memory_space=pltpu.HBM)


def shape(dims, kind):
    return jax.ShapeDtypeStruct(dims, kind)


def in_hbm(x):
    return pltpu.with_memory_space_constraint(x, pltpu.HBM)


def grant(mib):
    return pltpu.CompilerParams(vmem_limit_bytes=mib * MIB)


def cost(flops, size):
    return pl.CostEstimate(flops=flops, bytes_accessed=size, transcendentals=0)


def tiles(groups, step=STEP):
    found, place = [], 0
    for begin, end in runs(groups):
        for at in range(begin * GROUP, end * GROUP, step):
            size = min(step, end * GROUP - at)
            found.append((at, place, size))
            place += size
    return found


def core_of():
    return lax.rem(lax.axis_index("task"), 2)


def columns(begin, size, side, span):
    return pl.ds(pl.multiple_of(side * span + begin, GROUP), size)


def project(values, factors, groups, resident, mine):
    tasks, ranks = factors.shape
    span, width = values.shape[1] // 2, len(groups) * GROUP
    cuts = tiles(groups, 2 * STEP if resident else width)

    kind = jnp.float32 if mine else jnp.bfloat16

    def body(f_hbm, v_hbm, out, v_ref, f_ref, sems):
        side = core_of() if mine else 1 - core_of()
        first = pltpu.make_async_copy(f_hbm, f_ref, sems.at[len(cuts)])
        first.start()
        copies = [] if resident else [
            pltpu.make_async_copy(v_hbm.at[:, columns(at, size, side, span)], v_ref.at[:, pl.ds(place, size)], sems.at[i])
            for i, (at, place, size) in enumerate(cuts)
        ]
        for copy in copies:
            copy.start()
        first.wait()
        turned = f_ref[...].astype(jnp.float32).T.astype(jnp.bfloat16)
        for i, (at, place, size) in enumerate(cuts):
            s = slice(place, place + size)
            if resident:
                field = v_hbm[:, columns(at, size, side, span)]
            else:
                copies[i].wait()
                field = v_ref[:, s]
            out[:, s] = jnp.dot(turned, field, preferred_element_type=jnp.float32).astype(kind)

    return pl.pallas_call(
        body,
        out_shape=shape((ranks, width), kind),
        in_specs=[HBM, VM if resident else HBM],
        out_specs=VM,
        scratch_shapes=[
            pltpu.VMEM((16, GROUP) if resident else (tasks, width), values.dtype),
            pltpu.VMEM(factors.shape, factors.dtype),
            pltpu.SemaphoreType.DMA((len(cuts) + 1,)),
        ],
        compiler_params=grant(14),
        cost_estimate=cost(2 * tasks * ranks * width, tasks * width * 2),
        name="project",
    )(in_hbm(factors), values if resident else in_hbm(values))


def make_tables(jitter, neighbours, scales, nugget):
    span, owner, lat = jitter.shape[1] // 2, neighbours.shape[1], scales.shape[1]

    tasks = nugget.shape[1]

    def body(j_hbm, n_hbm, s_hbm, g_hbm, j_out, gap_out, beta_out, noise_out, n_ref, s_ref, g_ref, gap_ref, sems):
        core = core_of()
        copies = [
            pltpu.make_async_copy(j_hbm.at[:, columns(0, span, core, span)], j_out, sems.at[0]),
            pltpu.make_async_copy(n_hbm, n_ref, sems.at[1]),
            pltpu.make_async_copy(s_hbm, s_ref, sems.at[2]),
            pltpu.make_async_copy(g_hbm, g_ref, sems.at[3]),
        ]
        for copy in copies:
            copy.start()
        for copy in copies:
            copy.wait()
        noise_out[...] = jnp.broadcast_to(jnp.broadcast_to(g_ref[...], (8, tasks)).T[:, :1], (tasks, GROUP))
        lane = lax.broadcasted_iota(jnp.int32, (owner, GROUP), 1)
        for parity in range(2):
            cut = jnp.where(n_ref[parity + 1 : parity + 2, :] < 0, FAR_AWAY, 0.0)
            column = jnp.broadcast_to(cut, (8, owner)).T[:, :1]
            gap_ref[parity] = jnp.where((lane < HALF) == (parity == 0), jnp.broadcast_to(column, (owner, GROUP)), 0.0)
            mine = pl.multiple_of(core * (owner // 2), owner // 2)
            gap_out[parity] = gap_ref[parity, pl.ds(mine, owner // 2), :]
        scale = s_ref[...]
        which = lax.broadcasted_iota(jnp.int32, scale.shape, 1)
        beta = 1.0 / (KAPPA * scale * scale)
        for q in range(lat):
            value = jnp.sum(jnp.where(which == q, beta, 0.0), axis=1, keepdims=True)
            beta_out[8 * q : 8 * q + 8, :] = jnp.broadcast_to(value, (8, GROUP))

    return pl.pallas_call(
        body,
        out_shape=(
            shape((2, span), jitter.dtype),
            shape((2, owner // 2, GROUP), jnp.float32),
            shape((8 * lat, GROUP), jnp.float32),
            shape((tasks, GROUP), jnp.float32),
        ),
        in_specs=[HBM] * 4,
        out_specs=(VM, VM, VM, VM),
        scratch_shapes=[
            pltpu.VMEM(neighbours.shape, neighbours.dtype),
            pltpu.VMEM(scales.shape, scales.dtype),
            pltpu.VMEM(nugget.shape, nugget.dtype),
            pltpu.VMEM((2, owner, GROUP), jnp.float32),
            pltpu.SemaphoreType.DMA((4,)),
        ],
        compiler_params=grant(2),
        cost_estimate=cost(jitter.size, 4 * jitter.size),
        name="make_tables",
    )(in_hbm(jitter), in_hbm(neighbours), in_hbm(scales), in_hbm(nugget))


def add_cores(own, received, held, chunks):
    ranks = own.shape[0]

    def body(own_ref, got_ref, *outs):
        for groups, out in zip(chunks, outs):
            for begin, end in runs(groups):
                place = groups.index(begin) * GROUP
                s = slice(held.index(begin) * GROUP, held.index(end - 1) * GROUP + GROUP)
                total = own_ref[:, s] + got_ref[:, s].astype(jnp.float32)
                out[:, place : place + (end - begin) * GROUP] = total.astype(jnp.bfloat16)

    return pl.pallas_call(
        body,
        out_shape=[shape((ranks, len(groups) * GROUP), jnp.bfloat16) for groups in chunks],
        in_specs=[VM, VM],
        out_specs=[VM] * len(chunks),
        compiler_params=grant(8),
        cost_estimate=cost(own.size, own.size * 6),
        name="add_cores",
    )(own, received)


def take_edges(first, last, offsets):
    ranks = first.shape[0]

    def body(first_ref, last_ref, j_ref, *outs):
        for out, source, s in ((outs[0], first_ref, slice(0, GROUP)), (outs[1], last_ref, slice(-GROUP, None))):
            out[:ranks, :] = source[:, s]
            out[ranks:, :] = jnp.zeros((EDGE_ROWS, GROUP), jnp.bfloat16)
            out[ranks : ranks + 2, :] = j_ref[:, s]

    return pl.pallas_call(
        body,
        out_shape=[shape((ranks + EDGE_ROWS, GROUP), jnp.bfloat16)] * 2,
        in_specs=[VM] * 3,
        out_specs=[VM] * 2,
        compiler_params=grant(3),
        cost_estimate=cost(first.size, first.size),
        name="take_edges",
    )(first, last, offsets)


def close_ring(from_left, from_right, share):
    half, width = share.shape

    def body(left_ref, right_ref, share_ref, out, offsets):
        first_half = lax.broadcasted_iota(jnp.int32, (1, GROUP), 1) < HALF
        out[:, :width] = share_ref[...]
        out[:, width:] = jnp.where(first_half, right_ref[:half, :], left_ref[:half, :])
        offsets[...] = jnp.where(first_half, right_ref[half:, :], left_ref[half:, :])

    return pl.pallas_call(
        body,
        out_shape=(shape((half, width + GROUP), share.dtype), shape((EDGE_ROWS, GROUP), share.dtype)),
        in_specs=[VM, VM, VM],
        out_specs=(VM, VM),
        compiler_params=grant(2),
        cost_estimate=cost(share.size, 4 * share.size),
        name="close_ring",
    )(from_left, from_right, share)


def fill_blocks(region, groups, j_ref, gap_ref, beta_ref, edge_ref, k_ref):
    lat = beta_ref.shape[0] // 8
    rows = GROUP + REACH
    wide = 2 * GROUP
    sub = lax.broadcasted_iota(jnp.int32, (8, wide), 0)
    lane = lax.broadcasted_iota(jnp.int32, (8, wide), 1)
    row, col = ((lane >> 4).astype(jnp.float32), (lane & (SIDE - 1)).astype(jnp.float32))
    corner = lane >= GROUP
    past_row = jnp.where(corner, row - 11.0, row)
    zero = jnp.zeros_like(row)
    far_base = (
        jnp.where(sub == 1, past_row, jnp.where(sub == 4, row, jnp.where(sub >= 6, 1.0, zero))),
        jnp.where((sub == 1) | (sub == 4), col, jnp.where(sub >= 6, 1.0, zero)),
    )
    sub_1, lane_1 = sub[:, :GROUP], lane[:, :GROUP]
    meets = jnp.where((sub_1 < 3) == (lane_1 < HALF), 1.0, 0.0)
    own_base = tuple(jnp.where(sub_1 < 6, meets, -base[:, :GROUP]) for base in (row, col))
    none = jnp.zeros((8, GROUP), jnp.float32)
    first_half = lax.broadcasted_iota(jnp.int32, (1, GROUP), 1) < HALF
    scale = [beta_ref[8 * q : 8 * q + 1, :] for q in range(lat)]

    def offsets_of(b):
        if isinstance(b, int):
            return j_ref[:, b * GROUP : (b + 1) * GROUP].astype(jnp.float32)
        return j_ref[:, pl.ds(pl.multiple_of(b * GROUP, GROUP), GROUP)].astype(jnp.float32)

    def eight(x):
        return jnp.broadcast_to(x, (8, GROUP))

    def block(b, parity, slot):
        here = offsets_of(b)
        before = edge_ref[:2, :].astype(jnp.float32) if isinstance(b, int) and b == 0 else offsets_of(b - 1)
        after = edge_ref[:2, :].astype(jnp.float32) if isinstance(b, int) and b == groups - 1 else offsets_of(b + 1)
        gap = eight(gap_ref[parity, pl.ds(b // 2, 1), :])
        far, own = [], []
        for axis in range(2):
            mine = eight(here[axis : axis + 1])
            past = pltpu.roll(eight(before[axis : axis + 1]), REACH, 1)
            coming = eight(after[axis : axis + 1])
            base = far_base[axis]
            left = jnp.where((sub_1 == 0) | (sub_1 == 3), mine, base[:, :GROUP])
            right = jnp.where(sub_1 == 0, past, jnp.where(sub_1 == 3, coming, base[:, GROUP:]))
            if axis == 0 and parity == 0:
                right = jnp.where(sub_1 == 2, gap, right)
            if axis == 0 and parity == 1:
                right = jnp.where(sub_1 == 5, pltpu.roll(gap, HALF, 1), right)
            far.append(jnp.concatenate([left, right], axis=1))
            own.append(jnp.where(sub_1 == 6, -mine, own_base[axis]))
        left = jnp.concatenate(far, axis=0).T[:rows].astype(jnp.bfloat16)
        right = jnp.concatenate(
            [jnp.concatenate([own[0], none], axis=1), jnp.concatenate([none, own[1]], axis=1)], axis=0
        ).astype(jnp.bfloat16)
        away = jnp.dot(left, right, preferred_element_type=jnp.float32)
        across, sideways = away[:, :GROUP], away[:, GROUP:]
        distance = across * across + sideways * sideways
        for q in range(lat):
            u = jnp.maximum(1.0 / KAPPA - scale[q] * distance, 0.0)
            weight = (u * u * u * (4.0 * KAPPA**3 - u)).astype(jnp.bfloat16)
            s = slice(q * GROUP, (q + 1) * GROUP)
            blank = jnp.zeros((REACH, GROUP), jnp.bfloat16)
            k_ref[slot, :GROUP, s] = weight[:GROUP]
            k_ref[slot, GROUP : GROUP + REACH, s] = jnp.where(first_half, blank, weight[GROUP:])
            k_ref[slot, wide - REACH :, s] = jnp.where(first_half, weight[GROUP:], blank)
        k_ref[slot, GROUP + REACH : wide - REACH, :] = jnp.zeros((GROUP - 2 * REACH, lat * GROUP), jnp.bfloat16)

    count = 4
    for begin, end in runs(region):
        slot = region.index(begin)
        low, high = begin + (begin == 0), end - (end == groups)
        low = min(low + low % 2, end)
        for b in range(begin, low):
            block(b, b % 2, slot + b - begin)
        whole = (high - low) // count

        def several(i, carry, low=low, shift=slot - begin):
            for m in range(count):
                b = low + i * count + m
                block(b, m % 2, b + shift)
            return carry

        if whole > 1:
            lax.fori_loop(0, whole, several, 0)
        else:
            whole = 0
        for b in range(low + whole * count, end):
            block(b, b % 2, slot + b - begin)


def kernel_blocks(tables, edges, region, groups):
    args = list(tables) + ([edges] if edges is not None else [])

    def body(*refs):
        fill_blocks(region, groups, *refs[:3], refs[3], refs[-1])

    return pl.pallas_call(
        body,
        out_shape=block_shape(tables, region),
        in_specs=[VM] * len(args),
        out_specs=VM,
        compiler_params=grant(6),
        cost_estimate=block_cost(tables, region),
        name="kernel_blocks",
    )(*args)


def block_shape(tables, region):
    return shape((len(region), 2 * GROUP, tables[2].shape[0] // 8 * GROUP), jnp.bfloat16)


def block_cost(tables, region):
    size = block_shape(tables, region).size
    return cost(30 * size, 2 * size)


def smooth(kernels, region, pieces, lat, rank, groups):
    half = lat * rank
    owners = [(k, m) for k, kernel in enumerate(kernels) for m in range(kernel.shape[0])]

    def body(*refs):
        k_refs, refs = refs[: len(kernels)], refs[len(kernels) :]
        out = refs[-1]
        first_half = lax.broadcasted_iota(jnp.int32, (1, GROUP), 1) < HALF

        def part(group, which, rows):
            group = groups if group < 0 else group
            for n, (held, _) in enumerate(pieces):
                if group in held:
                    at = held.index(group) * GROUP
                    return refs[2 * n + which][rows, at : at + GROUP]

        for n, b in enumerate(region):
            for q in range(lat):
                rows = slice(q * rank, (q + 1) * rank)
                sides = [
                    jnp.concatenate(
                        [part(b, w, rows), jnp.where(first_half, part(b + 1, w, rows), part(b - 1, w, rows))], axis=1
                    )
                    for w in range(2)
                ]
                total = jnp.dot(
                    jnp.concatenate(sides, axis=0),
                    k_refs[owners[n][0]][owners[n][1], :, q * GROUP : (q + 1) * GROUP],
                    preferred_element_type=jnp.float32,
                )
                out[rows, n * GROUP : (n + 1) * GROUP] = (total[:rank] + total[rank:]).astype(jnp.bfloat16)

    arrays = [a for _, pair in pieces for a in pair]
    count = len(region) * GROUP
    return pl.pallas_call(
        body,
        out_shape=shape((half, count), jnp.bfloat16),
        in_specs=[VM] * (len(kernels) + len(arrays)),
        out_specs=VM,
        compiler_params=grant(8),
        cost_estimate=cost(8 * half * GROUP * count, 4 * GROUP * lat * count),
        name="smooth",
    )(*kernels, *arrays)


def mix(smoothed, factors, noise, values, product, region, mine, more=None):
    tasks = factors.shape[0]
    span, width = values.shape[1] // 2, len(region) * GROUP
    cuts = tiles(region, GROUP)

    def body(s_ref, f_ref, g_ref, v_ref, *rest):
        o_buf, sems = rest[-2:]
        o_hbm = rest[-4] if more else rest[-3]
        side = core_of() if mine else 1 - core_of()
        copies = []
        for i, (at, place, size) in enumerate(cuts):
            s, p = slice(place, place + size), columns(at, size, side, span)
            mixed = jnp.dot(f_ref[...], s_ref[:, s], preferred_element_type=jnp.float32)
            o_buf[:, s] = mixed + g_ref[...] * v_ref[:, p].astype(jnp.float32)
            copies.append(pltpu.make_async_copy(o_buf.at[:, pl.ds(place, size)], o_hbm.at[:, p], sems.at[i]))
            copies[-1].start()
        if more:
            fill_blocks(more[2], more[3], *rest[:3], rest[3], rest[-3])
        for copy in copies:
            copy.wait()

    args = [smoothed, factors, noise, values]
    out, out_specs = [shape(values.shape, jnp.float32)], [HBM]
    price = cost(2 * tasks * factors.shape[1] * width, tasks * width * 4)
    if more:
        args += list(more[0]) + ([more[1]] if more[1] is not None else [])
        out.append(block_shape(more[0], more[2]))
        out_specs.append(VM)
        built = block_cost(more[0], more[2])
        price = cost(price.flops + built.flops, price.bytes_accessed + built.bytes_accessed)
    specs = [VM] * len(args)
    alias = {}
    if product is not None:
        alias = {len(args): 0}
        args.append(product)
        specs.append(HBM)
    return pl.pallas_call(
        body,
        out_shape=out,
        in_specs=specs,
        out_specs=out_specs,
        scratch_shapes=[pltpu.VMEM((tasks, width), jnp.float32), pltpu.SemaphoreType.DMA((len(cuts),))],
        input_output_aliases=alias,
        compiler_params=grant(12),
        cost_estimate=price,
        name="mix",
    )(*args)


def runs(groups):
    found = []
    for g in groups:
        if found and found[-1][1] == g:
            found[-1][1] = g + 1
        else:
            found.append([g, g + 1])
    return found


def partners(size, bit):
    return [(i, i ^ bit) for i in range(size)]


def sum_fields(share, size):
    bit, other = 2, None
    while bit < size:
        if other is not None:
            share = (share.astype(jnp.float32) + other.astype(jnp.float32)).astype(jnp.bfloat16)
        other = lax.ppermute(share, "task", partners(size, bit))
        bit *= 2
    return share, other


def plan(groups):
    cuts = [1] + [groups * n // 32 for n in CUTS]
    regions = [list(range(a, b)) for a, b in zip(cuts[:-1], cuts[1:])]
    regions.append(list(range(cuts[-1], groups)) + [0])
    starts = [0] + [c + 1 for c in cuts[1:]] + [groups]
    chunks = [list(range(a, b)) for a, b in zip(starts[:-1], starts[1:])]
    return regions, chunks


def steps_of(values, factors, jitter, length_scales, nugget, neighbours):
    peers, blocks = lax.axis_size("task"), lax.axis_size("site")
    lat = length_scales.shape[0]
    rank = factors.shape[1] // lat
    groups = values.shape[1] // (2 * GROUP)
    regions, chunks = plan(groups)
    rest = [g for chunk in chunks[1:] for g in chunk]
    send = project(values, factors, chunks[0], False, False)
    received = lax.ppermute(send, "task", partners(peers, 1))
    own = project(values, factors, chunks[0], False, True)
    *tables, noise = make_tables(jitter, neighbours.T, length_scales.reshape(1, -1), nugget.reshape(1, -1))
    (share,) = add_cores(own, received, chunks[0], chunks[:1])
    sums = [sum_fields(share, peers)]
    send = project(values, factors, rest, True, False)
    own_rest = project(values, factors, rest, True, True)
    received = lax.ppermute(send, "task", partners(peers, 1))
    shares = add_cores(own_rest, received, rest, chunks[1:])
    for part in shares[:-1]:
        sums.append(sum_fields(part, peers))
    left_edge, right_edge = take_edges(share, shares[-1], tables[0])
    ring = [[s * peers + t + c for s in range(blocks) for c in range(2)] for t in range(0, peers, 2)]
    up = [(r[i], r[(i + 1) % len(r)]) for r in ring for i in range(len(r))]
    down = [(j, i) for i, j in up]
    from_left = lax.ppermute(right_edge, ("site", "task"), up)
    from_right = lax.ppermute(left_edge, ("site", "task"), down)
    last, outside = close_ring(from_left, from_right, shares[-1])
    sums.append(sum_fields(last, peers))
    held_groups = chunks[:-1] + [chunks[-1] + [groups]]

    final = len(regions) - 1
    middle = len(regions[1]) // 2
    parts = {"mix0": regions[1][:middle], "mix0b": regions[1][middle:], "mix1": regions[2], "mix1b": regions[3]}
    kernels = [[] for _ in regions]
    kernels[0].append(kernel_blocks(tables, None, regions[0], groups))

    product = None
    for n, region in enumerate(regions):
        pieces = [(held_groups[n], sums[n])]
        if n > 0:
            pieces.append((held_groups[n - 1], sums[n - 1]))
        if n == final:
            pieces.append((held_groups[0], sums[0]))
        smoothed = smooth(kernels[n], region, pieces, lat, rank, groups)
        other = lax.ppermute(smoothed, "task", partners(peers, 1))
        for name, rows, mine in ((f"mix{n}", smoothed, True), (f"mix{n}b", other, False)):
            part = parts.get(name)
            more = part and (tables, outside if part is regions[final] else None, part, groups)
            product, *built = mix(rows, factors, noise, values, product, region, mine, more)
            if built:
                kernels[1 if part[0] in regions[1] else regions.index(part)].append(built[0])
    return product


def solution(mesh):
    return jax.shard_map(
        steps_of,
        mesh=mesh,
        in_specs=(
            P("task", "site"),
            P("task", None),
            P(None, "site"),
            P(),
            P("task"),
            P("site", None),
        ),
        out_specs=P("task", "site"),
        check_vma=False,
    )
```

```python
import jax
import jax.numpy as jnp
from jax import lax
from jax.experimental import pallas as pl
from jax.experimental.pallas import tpu as pltpu
from jax.sharding import PartitionSpec as P


SIDE = 16
GROUP = 128
HALF = GROUP // 2
REACH = 3 * SIDE
KAPPA = 3.0**-0.25
FAR_AWAY = 1024.0
STEP = 512
EDGE_ROWS = 16
MIB = 1 << 20
CUTS = (6, 20, 26)

VM = pl.BlockSpec(memory_space=pltpu.VMEM)
HBM = pl.BlockSpec(memory_space=pltpu.HBM)


def shape(dims, kind):
    return jax.ShapeDtypeStruct(dims, kind)


def in_hbm(x):
    return pltpu.with_memory_space_constraint(x, pltpu.HBM)


def grant(mib):
    return pltpu.CompilerParams(vmem_limit_bytes=mib * MIB)


def cost(flops, size):
    return pl.CostEstimate(flops=flops, bytes_accessed=size, transcendentals=0)


def tiles(groups, step=STEP):
    found, place = [], 0
    for begin, end in runs(groups):
        for at in range(begin * GROUP, end * GROUP, step):
            size = min(step, end * GROUP - at)
            found.append((at, place, size))
            place += size
    return found


def core_of():
    return lax.rem(lax.axis_index("task"), 2)


def columns(begin, size, side, span):
    return pl.ds(pl.multiple_of(side * span + begin, GROUP), size)


def project(values, factors, groups, resident, mine):
    tasks, ranks = factors.shape
    span, width = values.shape[1] // 2, len(groups) * GROUP
    cuts = tiles(groups, 2 * STEP if resident else width)

    kind = jnp.float32 if mine else jnp.bfloat16

    def body(f_hbm, v_hbm, out, v_ref, f_ref, sems):
        side = core_of() if mine else 1 - core_of()
        first = None if resident else pltpu.make_async_copy(f_hbm, f_ref, sems.at[len(cuts)])
        if first:
            first.start()
        copies = [] if resident else [
            pltpu.make_async_copy(v_hbm.at[:, columns(at, size, side, span)], v_ref.at[:, pl.ds(place, size)], sems.at[i])
            for i, (at, place, size) in enumerate(cuts)
        ]
        for copy in copies:
            copy.start()
        if first:
            first.wait()
        turned = (f_ref if first else f_hbm)[...].astype(jnp.float32).T.astype(jnp.bfloat16)
        for i, (at, place, size) in enumerate(cuts):
            s = slice(place, place + size)
            if resident:
                field = v_hbm[:, columns(at, size, side, span)]
            else:
                copies[i].wait()
                field = v_ref[:, s]
            out[:, s] = jnp.dot(turned, field, preferred_element_type=jnp.float32).astype(kind)

    return pl.pallas_call(
        body,
        out_shape=shape((ranks, width), kind),
        in_specs=[VM, VM] if resident else [HBM, HBM],
        out_specs=VM,
        scratch_shapes=[
            pltpu.VMEM((16, GROUP) if resident else (tasks, width), values.dtype),
            pltpu.VMEM(factors.shape, factors.dtype),
            pltpu.SemaphoreType.DMA((len(cuts) + 1,)),
        ],
        compiler_params=grant(14),
        cost_estimate=cost(2 * tasks * ranks * width, tasks * width * 2),
        name="project",
    )(*((factors, values) if resident else (in_hbm(factors), in_hbm(values))))


def make_tables(jitter, neighbours, scales, nugget):
    span, owner, lat = jitter.shape[1] // 2, neighbours.shape[1], scales.shape[1]

    tasks = nugget.shape[1]

    def body(j_hbm, n_hbm, s_hbm, g_hbm, j_out, gap_out, beta_out, noise_out, n_ref, s_ref, g_ref, gap_ref, sems):
        core = core_of()
        copies = [
            pltpu.make_async_copy(j_hbm.at[:, columns(0, span, core, span)], j_out, sems.at[0]),
            pltpu.make_async_copy(n_hbm, n_ref, sems.at[1]),
            pltpu.make_async_copy(s_hbm, s_ref, sems.at[2]),
            pltpu.make_async_copy(g_hbm, g_ref, sems.at[3]),
        ]
        for copy in copies:
            copy.start()
        for copy in copies:
            copy.wait()
        noise_out[...] = jnp.broadcast_to(jnp.broadcast_to(g_ref[...], (8, tasks)).T[:, :1], (tasks, GROUP))
        lane = lax.broadcasted_iota(jnp.int32, (owner, GROUP), 1)
        for parity in range(2):
            cut = jnp.where(n_ref[parity + 1 : parity + 2, :] < 0, FAR_AWAY, 0.0)
            column = jnp.broadcast_to(cut, (8, owner)).T[:, :1]
            gap_ref[parity] = jnp.where((lane < HALF) == (parity == 0), jnp.broadcast_to(column, (owner, GROUP)), 0.0)
            mine = pl.multiple_of(core * (owner // 2), owner // 2)
            gap_out[parity] = gap_ref[parity, pl.ds(mine, owner // 2), :]
        scale = s_ref[...]
        which = lax.broadcasted_iota(jnp.int32, scale.shape, 1)
        beta = 1.0 / (KAPPA * scale * scale)
        for q in range(lat):
            value = jnp.sum(jnp.where(which == q, beta, 0.0), axis=1, keepdims=True)
            beta_out[8 * q : 8 * q + 8, :] = jnp.broadcast_to(value, (8, GROUP))

    return pl.pallas_call(
        body,
        out_shape=(
            shape((2, span), jitter.dtype),
            shape((2, owner // 2, GROUP), jnp.float32),
            shape((8 * lat, GROUP), jnp.float32),
            shape((tasks, GROUP), jnp.float32),
        ),
        in_specs=[HBM] * 4,
        out_specs=(VM, VM, VM, VM),
        scratch_shapes=[
            pltpu.VMEM(neighbours.shape, neighbours.dtype),
            pltpu.VMEM(scales.shape, scales.dtype),
            pltpu.VMEM(nugget.shape, nugget.dtype),
            pltpu.VMEM((2, owner, GROUP), jnp.float32),
            pltpu.SemaphoreType.DMA((4,)),
        ],
        compiler_params=grant(2),
        cost_estimate=cost(jitter.size, 4 * jitter.size),
        name="make_tables",
    )(in_hbm(jitter), in_hbm(neighbours), in_hbm(scales), in_hbm(nugget))


def add_cores(own, received, held, chunks):
    ranks = own.shape[0]

    def body(own_ref, got_ref, *outs):
        for groups, out in zip(chunks, outs):
            for begin, end in runs(groups):
                place = groups.index(begin) * GROUP
                s = slice(held.index(begin) * GROUP, held.index(end - 1) * GROUP + GROUP)
                total = own_ref[:, s] + got_ref[:, s].astype(jnp.float32)
                out[:, place : place + (end - begin) * GROUP] = total.astype(jnp.bfloat16)

    return pl.pallas_call(
        body,
        out_shape=[shape((ranks, len(groups) * GROUP), jnp.bfloat16) for groups in chunks],
        in_specs=[VM, VM],
        out_specs=[VM] * len(chunks),
        compiler_params=grant(8),
        cost_estimate=cost(own.size, own.size * 6),
        name="add_cores",
    )(own, received)


def take_edges(first, last, offsets):
    ranks = first.shape[0]

    def body(first_ref, last_ref, j_ref, *outs):
        for out, source, s in ((outs[0], first_ref, slice(0, GROUP)), (outs[1], last_ref, slice(-GROUP, None))):
            out[:ranks, :] = source[:, s]
            out[ranks:, :] = jnp.zeros((EDGE_ROWS, GROUP), jnp.bfloat16)
            out[ranks : ranks + 2, :] = j_ref[:, s]

    return pl.pallas_call(
        body,
        out_shape=[shape((ranks + EDGE_ROWS, GROUP), jnp.bfloat16)] * 2,
        in_specs=[VM] * 3,
        out_specs=[VM] * 2,
        compiler_params=grant(3),
        cost_estimate=cost(first.size, first.size),
        name="take_edges",
    )(first, last, offsets)


def close_ring(from_left, from_right, share):
    half, width = share.shape

    def body(left_ref, right_ref, share_ref, out, offsets):
        first_half = lax.broadcasted_iota(jnp.int32, (1, GROUP), 1) < HALF
        out[:, :width] = share_ref[...]
        out[:, width:] = jnp.where(first_half, right_ref[:half, :], left_ref[:half, :])
        offsets[...] = jnp.where(first_half, right_ref[half:, :], left_ref[half:, :])

    return pl.pallas_call(
        body,
        out_shape=(shape((half, width + GROUP), share.dtype), shape((EDGE_ROWS, GROUP), share.dtype)),
        in_specs=[VM, VM, VM],
        out_specs=(VM, VM),
        compiler_params=grant(2),
        cost_estimate=cost(share.size, 4 * share.size),
        name="close_ring",
    )(from_left, from_right, share)


def fill_blocks(region, groups, j_ref, gap_ref, beta_ref, edge_ref, k_ref):
    lat = beta_ref.shape[0] // 8
    rows = GROUP + REACH
    wide = 2 * GROUP
    sub = lax.broadcasted_iota(jnp.int32, (8, wide), 0)
    lane = lax.broadcasted_iota(jnp.int32, (8, wide), 1)
    row, col = ((lane >> 4).astype(jnp.float32), (lane & (SIDE - 1)).astype(jnp.float32))
    corner = lane >= GROUP
    past_row = jnp.where(corner, row - 11.0, row)
    zero = jnp.zeros_like(row)
    far_base = (
        jnp.where(sub == 1, past_row, jnp.where(sub == 4, row, jnp.where(sub >= 6, 1.0, zero))),
        jnp.where((sub == 1) | (sub == 4), col, jnp.where(sub >= 6, 1.0, zero)),
    )
    sub_1, lane_1 = sub[:, :GROUP], lane[:, :GROUP]
    meets = jnp.where((sub_1 < 3) == (lane_1 < HALF), 1.0, 0.0)
    own_base = tuple(jnp.where(sub_1 < 6, meets, -base[:, :GROUP]) for base in (row, col))
    none = jnp.zeros((8, GROUP), jnp.float32)
    first_half = lax.broadcasted_iota(jnp.int32, (1, GROUP), 1) < HALF
    scale = [beta_ref[8 * q : 8 * q + 1, :] for q in range(lat)]

    def offsets_of(b):
        if isinstance(b, int):
            return j_ref[:, b * GROUP : (b + 1) * GROUP].astype(jnp.float32)
        return j_ref[:, pl.ds(pl.multiple_of(b * GROUP, GROUP), GROUP)].astype(jnp.float32)

    def eight(x):
        return jnp.broadcast_to(x, (8, GROUP))

    def block(b, parity, slot):
        here = offsets_of(b)
        before = edge_ref[:2, :].astype(jnp.float32) if isinstance(b, int) and b == 0 else offsets_of(b - 1)
        after = edge_ref[:2, :].astype(jnp.float32) if isinstance(b, int) and b == groups - 1 else offsets_of(b + 1)
        gap = eight(gap_ref[parity, pl.ds(b // 2, 1), :])
        far, own = [], []
        for axis in range(2):
            mine = eight(here[axis : axis + 1])
            past = pltpu.roll(eight(before[axis : axis + 1]), REACH, 1)
            coming = eight(after[axis : axis + 1])
            base = far_base[axis]
            left = jnp.where((sub_1 == 0) | (sub_1 == 3), mine, base[:, :GROUP])
            right = jnp.where(sub_1 == 0, past, jnp.where(sub_1 == 3, coming, base[:, GROUP:]))
            if axis == 0 and parity == 0:
                right = jnp.where(sub_1 == 2, gap, right)
            if axis == 0 and parity == 1:
                right = jnp.where(sub_1 == 5, pltpu.roll(gap, HALF, 1), right)
            far.append(jnp.concatenate([left, right], axis=1))
            own.append(jnp.where(sub_1 == 6, -mine, own_base[axis]))
        left = jnp.concatenate(far, axis=0).T[:rows].astype(jnp.bfloat16)
        right = jnp.concatenate(
            [jnp.concatenate([own[0], none], axis=1), jnp.concatenate([none, own[1]], axis=1)], axis=0
        ).astype(jnp.bfloat16)
        away = jnp.dot(left, right, preferred_element_type=jnp.float32)
        across, sideways = away[:, :GROUP], away[:, GROUP:]
        distance = across * across + sideways * sideways
        for q in range(lat):
            u = jnp.maximum(1.0 / KAPPA - scale[q] * distance, 0.0)
            weight = (u * u * u * (4.0 * KAPPA**3 - u)).astype(jnp.bfloat16)
            s = slice(q * GROUP, (q + 1) * GROUP)
            blank = jnp.zeros((REACH, GROUP), jnp.bfloat16)
            k_ref[slot, :GROUP, s] = weight[:GROUP]
            k_ref[slot, GROUP : GROUP + REACH, s] = jnp.where(first_half, blank, weight[GROUP:])
            k_ref[slot, wide - REACH :, s] = jnp.where(first_half, weight[GROUP:], blank)
        k_ref[slot, GROUP + REACH : wide - REACH, :] = jnp.zeros((GROUP - 2 * REACH, lat * GROUP), jnp.bfloat16)

    count = 4
    for begin, end in runs(region):
        slot = region.index(begin)
        low, high = begin + (begin == 0), end - (end == groups)
        low = min(low + low % 2, end)
        for b in range(begin, low):
            block(b, b % 2, slot + b - begin)
        whole = (high - low) // count

        def several(i, carry, low=low, shift=slot - begin):
            for m in range(count):
                b = low + i * count + m
                block(b, m % 2, b + shift)
            return carry

        if whole > 1:
            lax.fori_loop(0, whole, several, 0)
        else:
            whole = 0
        for b in range(low + whole * count, end):
            block(b, b % 2, slot + b - begin)


def kernel_blocks(tables, edges, region, groups):
    args = list(tables) + ([edges] if edges is not None else [])

    def body(*refs):
        fill_blocks(region, groups, *refs[:3], refs[3], refs[-1])

    return pl.pallas_call(
        body,
        out_shape=block_shape(tables, region),
        in_specs=[VM] * len(args),
        out_specs=VM,
        compiler_params=grant(6),
        cost_estimate=block_cost(tables, region),
        name="kernel_blocks",
    )(*args)


def block_shape(tables, region):
    return shape((len(region), 2 * GROUP, tables[2].shape[0] // 8 * GROUP), jnp.bfloat16)


def block_cost(tables, region):
    size = block_shape(tables, region).size
    return cost(30 * size, 2 * size)


def smooth(kernels, region, pieces, lat, rank, groups):
    half = lat * rank
    owners = [(k, m) for k, kernel in enumerate(kernels) for m in range(kernel.shape[0])]

    def body(*refs):
        k_refs, refs = refs[: len(kernels)], refs[len(kernels) :]
        out = refs[-1]
        first_half = lax.broadcasted_iota(jnp.int32, (1, GROUP), 1) < HALF

        def part(group, which, rows):
            group = groups if group < 0 else group
            for n, (held, _) in enumerate(pieces):
                if group in held:
                    at = held.index(group) * GROUP
                    return refs[2 * n + which][rows, at : at + GROUP]

        for n, b in enumerate(region):
            for q in range(lat):
                rows = slice(q * rank, (q + 1) * rank)
                sides = [
                    jnp.concatenate(
                        [part(b, w, rows), jnp.where(first_half, part(b + 1, w, rows), part(b - 1, w, rows))], axis=1
                    )
                    for w in range(2)
                ]
                total = jnp.dot(
                    jnp.concatenate(sides, axis=0),
                    k_refs[owners[n][0]][owners[n][1], :, q * GROUP : (q + 1) * GROUP],
                    preferred_element_type=jnp.float32,
                )
                out[rows, n * GROUP : (n + 1) * GROUP] = (total[:rank] + total[rank:]).astype(jnp.bfloat16)

    arrays = [a for _, pair in pieces for a in pair]
    count = len(region) * GROUP
    return pl.pallas_call(
        body,
        out_shape=shape((half, count), jnp.bfloat16),
        in_specs=[VM] * (len(kernels) + len(arrays)),
        out_specs=VM,
        compiler_params=grant(8),
        cost_estimate=cost(8 * half * GROUP * count, 4 * GROUP * lat * count),
        name="smooth",
    )(*kernels, *arrays)


def mix(smoothed, factors, noise, values, product, region, mine, more=None):
    tasks = factors.shape[0]
    span, width = values.shape[1] // 2, len(region) * GROUP
    cuts = tiles(region, GROUP)

    def body(s_ref, f_ref, g_ref, v_ref, *rest):
        o_buf, sems = rest[-2:]
        o_hbm = rest[-4] if more else rest[-3]
        side = core_of() if mine else 1 - core_of()
        copies = []
        for i, (at, place, size) in enumerate(cuts):
            s, p = slice(place, place + size), columns(at, size, side, span)
            mixed = jnp.dot(f_ref[...], s_ref[:, s], preferred_element_type=jnp.float32)
            o_buf[:, s] = mixed + g_ref[...] * v_ref[:, p].astype(jnp.float32)
            copies.append(pltpu.make_async_copy(o_buf.at[:, pl.ds(place, size)], o_hbm.at[:, p], sems.at[i]))
            copies[-1].start()
        if more:
            fill_blocks(more[2], more[3], *rest[:3], rest[3], rest[-3])
        for copy in copies:
            copy.wait()

    args = [smoothed, factors, noise, values]
    out, out_specs = [shape(values.shape, jnp.float32)], [HBM]
    price = cost(2 * tasks * factors.shape[1] * width, tasks * width * 4)
    if more:
        args += list(more[0]) + ([more[1]] if more[1] is not None else [])
        out.append(block_shape(more[0], more[2]))
        out_specs.append(VM)
        built = block_cost(more[0], more[2])
        price = cost(price.flops + built.flops, price.bytes_accessed + built.bytes_accessed)
    specs = [VM] * len(args)
    alias = {}
    if product is not None:
        alias = {len(args): 0}
        args.append(product)
        specs.append(HBM)
    return pl.pallas_call(
        body,
        out_shape=out,
        in_specs=specs,
        out_specs=out_specs,
        scratch_shapes=[pltpu.VMEM((tasks, width), jnp.float32), pltpu.SemaphoreType.DMA((len(cuts),))],
        input_output_aliases=alias,
        compiler_params=grant(12),
        cost_estimate=price,
        name="mix",
    )(*args)


def runs(groups):
    found = []
    for g in groups:
        if found and found[-1][1] == g:
            found[-1][1] = g + 1
        else:
            found.append([g, g + 1])
    return found


def partners(size, bit):
    return [(i, i ^ bit) for i in range(size)]


def sum_fields(share, size):
    bit, other = 2, None
    while bit < size:
        if other is not None:
            share = (share.astype(jnp.float32) + other.astype(jnp.float32)).astype(jnp.bfloat16)
        other = lax.ppermute(share, "task", partners(size, bit))
        bit *= 2
    return share, other


def plan(groups):
    cuts = [1] + [groups * n // 32 for n in CUTS]
    regions = [list(range(a, b)) for a, b in zip(cuts[:-1], cuts[1:])]
    regions.append(list(range(cuts[-1], groups)) + [0])
    starts = [0] + [c + 1 for c in cuts[1:]] + [groups]
    chunks = [list(range(a, b)) for a, b in zip(starts[:-1], starts[1:])]
    return regions, chunks


def steps_of(values, factors, jitter, length_scales, nugget, neighbours):
    peers, blocks = lax.axis_size("task"), lax.axis_size("site")
    lat = length_scales.shape[0]
    rank = factors.shape[1] // lat
    groups = values.shape[1] // (2 * GROUP)
    regions, chunks = plan(groups)
    rest = [g for chunk in chunks[1:] for g in chunk]
    send = project(values, factors, chunks[0], False, False)
    received = lax.ppermute(send, "task", partners(peers, 1))
    own = project(values, factors, chunks[0], False, True)
    *tables, noise = make_tables(jitter, neighbours.T, length_scales.reshape(1, -1), nugget.reshape(1, -1))
    (share,) = add_cores(own, received, chunks[0], chunks[:1])
    sums = [sum_fields(share, peers)]
    send = project(values, factors, rest, True, False)
    own_rest = project(values, factors, rest, True, True)
    received = lax.ppermute(send, "task", partners(peers, 1))
    shares = add_cores(own_rest, received, rest, chunks[1:])
    for part in shares[:-1]:
        sums.append(sum_fields(part, peers))
    left_edge, right_edge = take_edges(share, shares[-1], tables[0])
    ring = [[s * peers + t + c for s in range(blocks) for c in range(2)] for t in range(0, peers, 2)]
    up = [(r[i], r[(i + 1) % len(r)]) for r in ring for i in range(len(r))]
    down = [(j, i) for i, j in up]
    from_left = lax.ppermute(right_edge, ("site", "task"), up)
    from_right = lax.ppermute(left_edge, ("site", "task"), down)
    last, outside = close_ring(from_left, from_right, shares[-1])
    sums.append(sum_fields(last, peers))
    held_groups = chunks[:-1] + [chunks[-1] + [groups]]

    final = len(regions) - 1
    middle = len(regions[1]) // 2
    parts = {"mix0": regions[1][:middle], "mix0b": regions[1][middle:], "mix1": regions[2], "mix1b": regions[3]}
    kernels = [[] for _ in regions]
    kernels[0].append(kernel_blocks(tables, None, regions[0], groups))

    product = None
    for n, region in enumerate(regions):
        pieces = [(held_groups[n], sums[n])]
        if n > 0:
            pieces.append((held_groups[n - 1], sums[n - 1]))
        if n == final:
            pieces.append((held_groups[0], sums[0]))
        smoothed = smooth(kernels[n], region, pieces, lat, rank, groups)
        other = lax.ppermute(smoothed, "task", partners(peers, 1))
        for name, rows, mine in ((f"mix{n}", smoothed, True), (f"mix{n}b", other, False)):
            part = parts.get(name)
            more = part and (tables, outside if part is regions[final] else None, part, groups)
            product, *built = mix(rows, factors, noise, values, product, region, mine, more)
            if built:
                kernels[1 if part[0] in regions[1] else regions.index(part)].append(built[0])
    return product


def solution(mesh):
    return jax.shard_map(
        steps_of,
        mesh=mesh,
        in_specs=(
            P("task", "site"),
            P("task", None),
            P(None, "site"),
            P(),
            P("task"),
            P("site", None),
        ),
        out_specs=P("task", "site"),
        check_vma=False,
    )
```
